512 devices in a mesh: rve: 128 (over z, y, core), blk: 4 (over x).
Axes of the slice: x: 4, y: 8, z: 8, core: 2. Of those that a mesh axis runs over, the one named last changes fastest.
Arguments:
- strain: bfloat16 [13824, 6], P(('rve', 'blk')), may hold values from -6 to 6
- fiber_coeff: bfloat16 [13824, 2048], P(('rve', 'blk')), may hold values from 0.049804688 to 0.8984375
- gradients: float32 [12, 13824], P(None, ('rve', 'blk')), may hold values from -6 to 6
- volume: float32 [13824], P(('rve', 'blk')), may hold values from 0.1 to 1
- corners: int32 [4, 13824], P(None, ('rve', 'blk')), may hold values from 0 to 65535, as said below
- rve_worker: int32 [13824], P(('rve', 'blk')), may hold values from 0 to 127, as said below
- rve_slot: int32 [13824], P(('rve', 'blk')), may hold values from 0 to 80, as said below
- slot_element: int32 [41472], P(('rve', 'blk')), may hold values from -1 to 13823, as said below
- state_table: float32 [41472, 3, 2048], P(('rve', 'blk')), may hold values from -6 to 6
- loading: bfloat16 [6, 3, 2048], replicated, may hold values from -6 to 6
- compliance: bfloat16 [2048, 2048], P('rve'), as said below
Outputs:
- new_states: float32 [41472, 3, 2048], P(('rve', 'blk'))
- node_forces: float32 [3, 65536], P(None, ('rve', 'blk'))
- node_blocks: float32 [9, 65536], P(None, ('rve', 'blk'))
The draws below stay inside these ranges and needn't reach their ends.
Inputs may be any that keep to these rules, and one draw needn't show every extreme that they name: `rve_worker`: counting the elements of one blk index, each worker number holds between 9 and 81 RVEs, the most reached by some worker; the elements of one aligned block of 27 that name one worker number are never more than 1, a count reached in every draw. `rve_slot`: A worker's RVEs fill its slots from 0 upward; no two elements share a worker and slot. `slot_element`: entry (w * 4 + b) * 81 + s holds e exactly when rve_worker[e] = w, (e // 27) % 4 = b and rve_slot[e] = s; every other entry is -1. The corners of elements in aligned block k of 27 elements are nodes k * 128 to (k + 2) * 128 - 1, and in the last block nodes k * 128 to (k + 1) * 128 - 1. `compliance`: Symmetric.
All inputs are finite; a program needn't handle non-finite values.
Results may differ from the reference program's by a relative error of at most 0.0023.
Values may be sent and summed in bfloat16 or wider, within the bound.
No kernel may reach another device: no remote copies, remote signals or barrier semaphores. Data moves between devices by JAX's collectives and lax.ppermute only.
A program may use at most 64 MiB of HBM per device.

```python
import math
import jax
import jax.numpy as jnp
import numpy as np
from jax import lax

NODES = 2048
ITERS = 3
ELEM_DEV = 27
NODE_DEV = 128
CAP = 81
ELEMS = 13824
NODES_ALL = 65536
N_RVE = 128
N_BLK = 4


def column_assignment(key, column):
    top_step = 2 * ELEM_DEV // 3
    key_order, key_steps = jax.random.split(jax.random.fold_in(jax.random.fold_in(key, 17), column))
    step_sizes = jax.random.randint(key_steps, ((N_RVE + 3) // 4,), 0, top_step + 1)
    step_sizes = step_sizes.at[0].set(top_step)
    position = jnp.arange(N_RVE)
    grouped = step_sizes[position // 4]
    lead = (position % 4 == 0) & (position + 3 < N_RVE)
    follow = (position % 4 != 0) & (position - position % 4 + 3 < N_RVE)
    by_position = jnp.where(lead, ELEM_DEV + 3 * grouped, jnp.where(follow, ELEM_DEV - grouped, ELEM_DEV))
    worker_loads = by_position[jax.random.permutation(key_order, N_RVE)]
    range_ends = jnp.cumsum(worker_loads)
    range_starts = range_ends - worker_loads
    return (worker_loads, range_starts, range_ends)


def assignment(key):
    return jax.vmap(lambda column: column_assignment(key, column))(jnp.arange(N_BLK))


def element_worker(key):
    worker_loads, range_starts, range_ends = assignment(key)
    element = jnp.arange(ELEMS)
    device = element // ELEM_DEV
    column = device % N_BLK
    row_index = device // N_BLK
    global_rank = element % ELEM_DEV * N_RVE + row_index
    chosen = jnp.sum(range_ends[column] <= global_rank[:, None], axis=1)
    return (chosen, global_rank - range_starts[column, chosen])


def draw_rve_worker(key, part):
    chosen, slots = element_worker(key)
    return chosen.astype(jnp.int32)


def draw_rve_slot(key, part):
    chosen, slots = element_worker(key)
    return slots.astype(jnp.int32)


def draw_slot_element(key, part):
    worker_loads, range_starts, range_ends = assignment(key)
    slot_index = jnp.arange(N_RVE * N_BLK * CAP)
    device = slot_index // CAP
    within = slot_index % CAP
    column = device % N_BLK
    owner_worker = device // N_BLK
    global_rank = range_starts[column, owner_worker] + within
    element = (global_rank % N_RVE * N_BLK + column) * ELEM_DEV + global_rank // N_RVE
    return jnp.where(within < worker_loads[column, owner_worker], element, -1).astype(jnp.int32)


def draw_corners(key, part):
    blocks_all = ELEMS // ELEM_DEV
    element = jnp.arange(ELEMS)
    home_block = element // ELEM_DEV
    reach = jnp.where(home_block == blocks_all - 1, NODE_DEV, 2 * NODE_DEV)
    offsets = jax.random.randint(jax.random.fold_in(key, 29), (4, ELEMS), 0, 2 * NODE_DEV) % reach[None, :]
    corner_row = jnp.arange(4)[:, None]
    offsets = jnp.where((corner_row == 0) & (element % ELEM_DEV == 0)[None, :], 0, offsets)
    offsets = jnp.where((corner_row == 3) & (element % ELEM_DEV == ELEM_DEV - 1)[None, :], reach[None, :] - 1, offsets)
    return (home_block[None, :] * NODE_DEV + offsets).astype(jnp.int32)


def draw_compliance(key, part):
    noise_key = jax.random.fold_in(key, 41)
    random_part = jax.random.normal(noise_key, (NODES, NODES), jnp.float32)
    symmetric = (random_part + random_part.T) * (0.3 / math.sqrt(2.0 * NODES))
    return (symmetric + jnp.eye(NODES, dtype=jnp.float32)).astype(jnp.bfloat16)


def shard_levels(stream_key, dims, cuts, low, high):
    def one(axis_at, blocks):
        heights = jax.random.uniform(jax.random.fold_in(jax.random.fold_in(stream_key, 6), axis_at), (blocks,), jnp.float32, low / len(cuts), high / len(cuts))
        return jnp.repeat(jnp.exp(heights), dims[axis_at] // blocks).reshape((-1,) + (1,) * (len(dims) - axis_at - 1))

    loudness = one(*cuts[0])
    for cut in cuts[1:]:
        loudness = loudness * one(*cut)
    return loudness


def centred(key, shape, width, limit, cuts=(), kind=jnp.bfloat16):
    result = jax.random.normal(key, shape, jnp.float32) * width
    if len(cuts) > 0:
        result = shard_levels(key, shape, cuts, -0.22, 0.18) * result
    return jnp.clip(result, min=-limit, max=limit).astype(kind)


def setup_inputs(seed: int = 0) -> dict:
    key_of = jax.random.split(jax.random.key(seed), 12)
    return {
        "strain": centred(key_of[0], (ELEMS, 6), 0.4, 6.0, ((0, 512),)),
        "fiber_coeff": jnp.clip(jnp.exp(math.log(0.8984375) - 2.892548 * jax.random.uniform(key_of[1], (ELEMS, NODES), jnp.float32) ** shard_levels(key_of[1], (ELEMS, NODES), ((0, 512),), -0.2, 0.2)), 0.049804688, 0.8984375).astype(jnp.bfloat16),
        "gradients": centred(key_of[2], (12, ELEMS), 1.0, 6.0, ((1, 512),), jnp.float32),
        "volume": jnp.clip(jnp.exp(math.log(1.0) - 2.3025851 * jax.random.uniform(key_of[3], (ELEMS,), jnp.float32) ** shard_levels(key_of[3], (ELEMS,), ((0, 512),), -0.2, 0.2)), 0.1, 1.0),
        "corners": draw_corners(jax.random.fold_in(key_of[11], 71), 0),
        "rve_worker": draw_rve_worker(jax.random.fold_in(key_of[11], 71), 0),
        "rve_slot": draw_rve_slot(jax.random.fold_in(key_of[11], 71), 0),
        "slot_element": draw_slot_element(jax.random.fold_in(key_of[11], 71), 0),
        "state_table": centred(key_of[8], (N_RVE * N_BLK * CAP, 3, NODES), 0.5, 6.0, ((0, 512),), jnp.float32),
        "loading": centred(key_of[9], (6, 3, NODES), 1.0, 6.0),
        "compliance": draw_compliance(jax.random.fold_in(key_of[11], 71), 0),
    }


highest = lax.Precision.HIGHEST


def strain_map():
    voigt_map = np.zeros((6, 3, 3), np.float32)
    for voigt_row, first_axis, second_axis in ((0, 0, 0), (1, 1, 1), (2, 2, 2), (3, 1, 2), (3, 2, 1), (4, 0, 2), (4, 2, 0), (5, 0, 1), (5, 1, 0)):
        voigt_map[voigt_row, first_axis, second_axis] = 1.0
    return jnp.asarray(voigt_map)


def micro_block(inputs, loading, compliance):
    strain_rows, coeff_rows, start_rows = inputs
    batch_rows = strain_rows.shape[0]
    forcing = jnp.dot(strain_rows, loading.reshape(6, 3 * NODES), preferred_element_type=jnp.float32).reshape(batch_rows, 3, NODES)
    current = start_rows
    for iteration in range(ITERS):
        pressure = (forcing - coeff_rows.astype(jnp.float32)[:, None, :] * jnp.tanh(current)).astype(jnp.bfloat16)
        current = jnp.dot(pressure.reshape(batch_rows * 3, NODES), compliance.T, preferred_element_type=jnp.float32).reshape(batch_rows, 3, NODES)
    return current


def reference(strain, fiber_coeff, gradients, volume, corners, rve_worker, rve_slot, slot_element, state_table, loading, compliance):
    blocks_all = ELEMS // ELEM_DEV
    column = ((jnp.arange(ELEMS) // ELEM_DEV) % N_BLK).astype(jnp.int32)
    flat_index = ((rve_worker * N_BLK + column) * CAP + rve_slot).astype(jnp.int32)
    starting = state_table[flat_index]
    blocks = (strain.reshape(blocks_all, ELEM_DEV, 6), fiber_coeff.reshape(blocks_all, ELEM_DEV, NODES), starting.reshape(blocks_all, ELEM_DEV, 3, NODES))
    finals = lax.map(lambda inputs: micro_block(inputs, loading, compliance), blocks).reshape(ELEMS, 3, NODES)
    occupied = slot_element >= 0
    picked = finals[jnp.maximum(slot_element, 0).astype(jnp.int32)]
    new_states = jnp.where(occupied[:, None, None], picked, state_table)
    mean_scale = 1.0 / (3 * NODES)
    load_float = loading.reshape(6, 3 * NODES).astype(jnp.float32)
    basis = jnp.dot(loading.reshape(18, NODES), compliance.T, preferred_element_type=jnp.float32).reshape(6, 3 * NODES)
    flat_state = finals.reshape(ELEMS, 3 * NODES)
    stress = jnp.dot(flat_state, load_float.T, precision=highest) * mean_scale
    fixed_part = jnp.dot(load_float, basis.T, precision=highest)
    products = (basis[:, None, :] * basis[None, :, :]).reshape(36, 3 * NODES)
    damping = (fiber_coeff.astype(jnp.float32)[:, None, :] * (1.0 - jnp.tanh(finals) ** 2)).reshape(ELEMS, 3 * NODES)
    tangent = (fixed_part.reshape(1, 36) - jnp.dot(damping, products.T, precision=highest)) * mean_scale
    gradient_rows = gradients.reshape(4, 3, ELEMS)
    bmatrix = jnp.einsum("vac,ich->ivah", strain_map(), gradient_rows, precision=highest)
    corner_force = volume * jnp.einsum("ivah,hv->iah", bmatrix, stress, precision=highest)
    corner_block = volume * jnp.einsum("ivah,hvw,iwbh->iabh", bmatrix, tangent.reshape(ELEMS, 6, 6), bmatrix, precision=highest)
    contrib = jnp.concatenate([corner_force, corner_block.reshape(4, 9, ELEMS)], axis=1)
    values = jnp.transpose(contrib, (0, 2, 1)).reshape(4 * ELEMS, 12)
    assembled = jax.ops.segment_sum(values, corners.reshape(4 * ELEMS).astype(jnp.int32), num_segments=NODES_ALL)
    return new_states, assembled[:, :3].T, assembled[:, 3:].T
```

```python
import functools

import jax
import jax.numpy as jnp
from jax import lax
from jax.experimental import pallas as pl
from jax.experimental.pallas import tpu as pltpu
from jax.sharding import PartitionSpec as P

ITERS = 3
NODE_DEV = 128
COMPS = 6
SLICE = 256

highest = lax.Precision.HIGHEST
f32 = jnp.float32
bf16 = jnp.bfloat16


def round_up(value, step):
    return (value + step - 1) // step * step


def dot_nn(left, right):
    return lax.dot_general(left, right, (((1,), (0,)), ((), ())), preferred_element_type=f32)


def dot_nt(left, right):
    return lax.dot_general(left, right, (((1,), (1,)), ((), ())), preferred_element_type=f32)


def split_dot_nt(left, right):
    left_head = left.astype(bf16)
    left_rest = (left - left_head.astype(f32)).astype(bf16)
    right_head = right.astype(bf16)
    right_rest = (right - right_head.astype(f32)).astype(bf16)
    return dot_nt(left_head, right_head) + (
        dot_nt(left_head, right_rest) + dot_nt(left_rest, right_head)
    )


def prepare_kernel(pick_ref, unit_ref, arrived_ref, loading_ref, state_ref, press_ref, forcing_ref, fiber_ref, still):
    cap = state_ref.shape[1]
    rows = pick_ref.shape[0]
    nodes = state_ref.shape[2]
    pick = pick_ref[...]
    strain = (dot_nn(pick, arrived_ref[:, nodes:]) + unit_ref[...]).astype(bf16)
    still[...] = jnp.zeros_like(still)
    for start in range(0, nodes, SLICE):
        cols = pl.ds(start, SLICE)
        fiber = dot_nn(pick, arrived_ref[:, cols])
        fiber_ref[:, cols] = fiber
        for a in range(3):
            still[0:cap, :] = state_ref[a, :, cols]
            forcing = dot_nn(strain, loading_ref[a, :, cols])
            forcing_ref[a, :, cols] = forcing
            press_ref[a * rows : (a + 1) * rows, cols] = (
                forcing - fiber * jnp.tanh(still[...])
            ).astype(bf16)


def solve_kernel(
    press_ref, forcing_ref, fiber_ref, loading_ref, occupied_ref, state_ref, network_hbm,
    table_ref, result_ref, network, pressure, current, products, sems,
):
    rows = fiber_ref.shape[0]
    nodes = fiber_ref.shape[1]
    cap = state_ref.shape[1]
    steps = nodes // SLICE

    def fetch(j):
        cols = pl.ds(j * SLICE, SLICE)
        return pltpu.make_async_copy(network_hbm.at[cols, :], network.at[cols, :], sems.at[j])

    for j in range(steps):
        fetch(j).start()
    for iteration in range(ITERS):
        source = press_ref if iteration == 0 else pressure.at[(iteration - 1) % 2]
        for j in range(steps):
            cols = pl.ds(j * SLICE, SLICE)
            if iteration == 0:
                fetch(j).wait()
            moved = dot_nt(source[...], network[cols, :])
            if iteration < ITERS - 1:
                fiber = fiber_ref[:, cols]
                for a in range(3):
                    block = moved[a * rows : (a + 1) * rows]
                    pressure[iteration % 2, a * rows : (a + 1) * rows, cols] = (
                        forcing_ref[a, :, cols] - fiber * jnp.tanh(block)
                    ).astype(bf16)
            else:
                for a in range(3):
                    current[a, :, cols] = moved[a * rows : (a + 1) * rows]
    stress = jnp.zeros((rows, 8), f32)
    damp = jnp.zeros((rows, 8 * COMPS), f32)
    fiber = fiber_ref[...]
    for a in range(3):
        state = current[a]
        head = state.astype(bf16)
        rest = (state - head.astype(f32)).astype(bf16)
        stress += dot_nt(head, loading_ref[a]) + dot_nt(rest, loading_ref[a])
        basis = current[a, cap : cap + COMPS, :]
        products[...] = jnp.zeros_like(products)
        for k in range(COMPS):
            products[8 * k : 8 * k + COMPS, :] = basis * basis[k : k + 1]
        bend = jnp.tanh(state)
        damp += split_dot_nt(fiber * (1.0 - bend * bend), products[...])
        table_ref[a] = jnp.where(
            occupied_ref[...] > 0, current[a, 0:cap, :], state_ref[a]
        )
    result_ref[:, 0 : 8 * COMPS] = damp
    result_ref[:, 8 * COMPS : 8 * COMPS + 8] = stress
    result_ref[:, 8 * COMPS + 8 :] = jnp.zeros((rows, result_ref.shape[1] - 8 * COMPS - 8), f32)


def corner_kernel(arrived_ref, pick_ref, fixed_ref, grad_ref, volume_ref, node_ref, out_ref, work, *, scale):
    got = lax.dot_general(
        arrived_ref[...], pick_ref[...], (((0,), (0,)), ((), ())),
        preferred_element_type=f32, precision=highest,
    )
    work[...] = got
    volume = volume_ref[...] * scale
    gx = grad_ref[0:1, :]
    gy = grad_ref[1:2, :]
    gz = grad_ref[2:3, :]

    def tangent(j):
        return fixed_ref[8 * j : 8 * j + 8, :] - work[8 * j : 8 * j + 8, :]

    t = [tangent(j) for j in range(COMPS)]
    columns = (
        t[0] * gx + t[4] * gz + t[5] * gy,
        t[1] * gy + t[3] * gz + t[5] * gx,
        t[2] * gz + t[3] * gy + t[4] * gx,
        work[8 * COMPS : 8 * COMPS + 8, :],
    )

    def rows(m):
        return (
            m[0:1] * gx + m[4:5] * gz + m[5:6] * gy,
            m[1:2] * gy + m[3:4] * gz + m[5:6] * gx,
            m[2:3] * gz + m[3:4] * gy + m[4:5] * gx,
        )

    blocks = [rows(m) for m in columns]
    contrib = [blocks[3][a] for a in range(3)] + [blocks[c][a] for a in range(3) for c in range(3)]
    lanes = work.shape[1]
    work[0:16, :] = jnp.zeros((16, lanes), f32)
    for r, row in enumerate(contrib):
        work[r : r + 1, :] = row * volume
    node = node_ref[...]
    spread = (lax.broadcasted_iota(jnp.int32, (2 * NODE_DEV, lanes), 0) == node).astype(f32)
    out_ref[...] = lax.dot_general(
        work[0:16, :], spread, (((1,), (1,)), ((), ())),
        preferred_element_type=f32, precision=highest,
    )


def from_behind(block, axis, distance):
    devices = range(lax.axis_size(axis))
    route = [(i - distance, i) for i in devices if i - distance in devices]
    return lax.ppermute(block, axis, route)


def body(
    strain, fiber_coeff, gradients, volume, corners, rve_worker, rve_slot, slot_element,
    state_table, loading, compliance,
):
    elems = strain.shape[0]
    workers = lax.axis_size("rve")
    columns = lax.axis_size("blk")
    cap = state_table.shape[0]
    nodes = compliance.shape[1]
    rows = round_up(cap + COMPS, 8)

    network = lax.all_gather(compliance, "rve", axis=0, tiled=True)

    worker_ids = jnp.arange(workers)
    send_pick = (worker_ids[:, None] == rve_worker[None, :]).astype(bf16)
    element_rows = jnp.concatenate([fiber_coeff, jnp.pad(strain, ((0, 0), (0, 128 - COMPS)))], axis=1)
    outgoing = jnp.dot(send_pick, element_rows)
    arrived = lax.all_to_all(outgoing, "rve", split_axis=0, concat_axis=0, tiled=True)

    occupied = slot_element >= 0
    home = jnp.where(occupied, slot_element // (elems * columns), -1)
    home_wide = jnp.pad(home, (0, rows - cap), constant_values=-1)
    slot_pick = (home_wide[:, None] == worker_ids[None, :])
    unit = (jnp.arange(rows)[:, None] - cap == jnp.arange(128)[None, :]).astype(f32)
    loading_rows = jnp.transpose(loading, (1, 0, 2))
    loading_wide = jnp.pad(loading_rows, ((0, 0), (0, 128 - COMPS), (0, 0)))
    loading_eight = jnp.pad(loading_rows, ((0, 0), (0, 8 - COMPS), (0, 0)))
    states = jnp.transpose(state_table, (1, 0, 2))

    press, forcing, fiber = pl.pallas_call(
        prepare_kernel,
        out_shape=(
            jax.ShapeDtypeStruct((3 * rows, nodes), bf16),
            jax.ShapeDtypeStruct((3, rows, nodes), f32),
            jax.ShapeDtypeStruct((rows, nodes), f32),
        ),
        scratch_shapes=[pltpu.VMEM((rows, SLICE), f32)],
        name="prepare",
    )(slot_pick.astype(bf16), unit, arrived, loading_wide, states)

    vmem = pl.BlockSpec(memory_space=pltpu.VMEM)
    table, result = pl.pallas_call(
        solve_kernel,
        out_shape=(
            jax.ShapeDtypeStruct((3, cap, nodes), f32),
            jax.ShapeDtypeStruct((rows, 128), f32),
        ),
        in_specs=[vmem] * 6 + [pl.BlockSpec(memory_space=pl.ANY)],
        out_specs=(vmem, vmem),
        scratch_shapes=[
            pltpu.VMEM((nodes, nodes), bf16),
            pltpu.VMEM((2, 3 * rows, nodes), bf16),
            pltpu.VMEM((3, rows, nodes), f32),
            pltpu.VMEM((8 * COMPS, nodes), f32),
            pltpu.SemaphoreType.DMA((nodes // SLICE,)),
        ],
        name="solve",
    )(press, forcing, fiber, loading_eight, occupied.astype(jnp.int32)[:, None], states, network)
    new_table = jnp.transpose(table, (1, 0, 2))

    backward = jnp.dot(slot_pick.astype(f32).T, result, precision=highest)
    returned = lax.all_to_all(backward, "rve", split_axis=0, concat_axis=0, tiled=True)

    fixed = result[cap : cap + COMPS, 8 * COMPS : 8 * COMPS + COMPS]
    fixed_rows = jnp.pad(fixed, ((0, 0), (0, 2))).reshape(8 * COMPS, 1)
    corner_pick = jnp.tile(send_pick.astype(f32), (1, 4))
    grad_rows = jnp.transpose(gradients.reshape(4, 3, elems), (1, 0, 2)).reshape(3, 4 * elems)
    device_rank = lax.axis_index("rve") * columns + lax.axis_index("blk")
    local_node = (corners - device_rank * NODE_DEV).reshape(1, 4 * elems)
    assembled = pl.pallas_call(
        functools.partial(corner_kernel, scale=1.0 / (3 * nodes)),
        out_shape=jax.ShapeDtypeStruct((16, 2 * NODE_DEV), f32),
        scratch_shapes=[pltpu.VMEM((128, 4 * elems), f32)],
        name="corners",
    )(returned, corner_pick, fixed_rows, grad_rows, jnp.tile(volume, 4)[None, :], local_node)
    own_rows = assembled[:, :NODE_DEV] + from_behind(assembled[:, NODE_DEV:], ("rve", "blk"), 1)
    return (new_table, own_rows[:3], own_rows[3:12])


def solution(mesh):
    both = ("rve", "blk")
    return jax.shard_map(
        body,
        mesh=mesh,
        in_specs=(
            P(both, None),
            P(both, None),
            P(None, both),
            P(both),
            P(None, both),
            P(both),
            P(both),
            P(both),
            P(both, None, None),
            P(),
            P("rve", None),
        ),
        out_specs=(P(both, None, None), P(None, both), P(None, both)),
        check_vma=False,
    )
```

```python
import functools

import jax
import jax.numpy as jnp
from jax import lax
from jax.experimental import pallas as pl
from jax.experimental.pallas import tpu as pltpu
from jax.sharding import PartitionSpec as P

ITERS = 3
NODE_DEV = 128
COMPS = 6
SLICE = 256
BLOCKS = 8
SENT = 5

highest = lax.Precision.HIGHEST
f32 = jnp.float32
bf16 = jnp.bfloat16


def round_up(value, step):
    return (value + step - 1) // step * step


def dot_nn(left, right):
    return lax.dot_general(left, right, (((1,), (0,)), ((), ())), preferred_element_type=f32)


def dot_nt(left, right):
    return lax.dot_general(left, right, (((1,), (1,)), ((), ())), preferred_element_type=f32)


def three_parts(value):
    head = value.astype(bf16)
    rest = value - head.astype(f32)
    middle = rest.astype(bf16)
    return head, middle, (rest - middle.astype(f32)).astype(bf16)


def prepare_kernel(pick_ref, unit_ref, arrived_ref, loading_ref, state_ref, press_ref, forcing_ref, fiber_ref, still):
    cap = state_ref.shape[1]
    rows = pick_ref.shape[0]
    nodes = state_ref.shape[2]
    pick = pick_ref[...]
    strain = (dot_nn(pick, arrived_ref[:, nodes:]) + unit_ref[...]).astype(bf16)
    still[...] = jnp.zeros_like(still)
    for start in range(0, nodes, SLICE):
        cols = pl.ds(start, SLICE)
        fiber = dot_nn(pick, arrived_ref[:, cols])
        fiber_ref[:, cols] = fiber
        for a in range(3):
            still[0:cap, :] = state_ref[a, :, cols]
            forcing = dot_nn(strain, loading_ref[a, :, cols])
            forcing_ref[a, :, cols] = forcing
            first = (forcing - fiber * jnp.tanh(still[...])).astype(bf16)
            press_ref[a * rows : (a + 1) * rows, cols] = first
            if nodes + start < press_ref.shape[1]:
                press_ref[a * rows : (a + 1) * rows, pl.ds(nodes + start, SLICE)] = first


def solve_kernel(
    side_ref, pick_ref, loading_ref, occupied_ref, press_hbm, forcing_hbm, fiber_hbm, state_hbm,
    mine_hbm, other_hbm, table_hbm, result_ref, back_ref,
    network, pressure, forcing, fiber, table, damp_sum, stress_sum, net_sems, in_sems, out_sems,
):
    rows = fiber.shape[0]
    nodes = fiber.shape[1]
    cap = table.shape[1]

    def fetch(i, side, source, k):
        return pltpu.make_async_copy(source.at[i], network.at[i, :, side], net_sems.at[i, k])

    inputs = (
        pltpu.make_async_copy(press_hbm, pressure.at[0], in_sems.at[0]),
        pltpu.make_async_copy(forcing_hbm, forcing, in_sems.at[1]),
        pltpu.make_async_copy(fiber_hbm, fiber, in_sems.at[2]),
        pltpu.make_async_copy(state_hbm, table, in_sems.at[3]),
    )
    inputs[0].start()
    arrival = [(1 + i) % BLOCKS for i in range(BLOCKS)]
    for side in range(2):

        @pl.when(side_ref[0] == side)
        def _():
            for i in arrival:
                fetch(i, side, mine_hbm, 0).start()
                fetch(i, 1 - side, other_hbm, 1).start()

    for copy in inputs[1:]:
        copy.start()

    def wait_network(i):
        fetch(i, 0, mine_hbm, 0).wait()
        fetch(i, 0, other_hbm, 1).wait()

    def net(i, start, blocks):
        cols = pl.ds(start * SLICE, blocks * SLICE)
        return network[i, :, :, :, cols].reshape(SLICE, blocks * SLICE)

    def stored(n):
        return pltpu.make_async_copy(
            table.at[:, :, pl.ds(n * SLICE, SLICE)],
            table_hbm.at[:, :, pl.ds(n * SLICE, SLICE)],
            out_sems.at[n],
        )

    damp_sum[...] = jnp.zeros_like(damp_sum)
    stress_sum[...] = jnp.zeros_like(stress_sum)
    inputs[0].wait()
    for i in arrival[:3]:
        wait_network(i)
    for iteration in range(ITERS):
        source = pressure.at[iteration]
        for step in range(BLOCKS):
            n = (step + 4) % BLOCKS
            cols = pl.ds(n * SLICE, SLICE)
            if iteration == 0 and step < BLOCKS - 3:
                wait_network(n)
            moved = dot_nt(source[:, pl.ds(n * SLICE, SENT * SLICE)], net(n, 0, SENT))
            for d in range(1, BLOCKS - SENT + 1):
                i = (n - d) % BLOCKS
                moved += dot_nn(source[:, pl.ds(i * SLICE, SLICE)], net(i, d, 1))
            if iteration == 0 and step == 0:
                inputs[1].wait()
                inputs[2].wait()
            damping = fiber[:, cols]
            bend = jnp.tanh(moved)
            if iteration < ITERS - 1:
                for a in range(3):
                    block = slice(a * rows, (a + 1) * rows)
                    value = (forcing[a, :, cols] - damping * bend[block]).astype(bf16)
                    pressure[iteration + 1, block, cols] = value
                    if n < SENT - 1:
                        pressure[iteration + 1, block, pl.ds(nodes + n * SLICE, SLICE)] = value
                continue
            if step == 0:
                inputs[3].wait()
            products = []
            for a in range(3):
                low = a * rows
                table[a, :, cols] = jnp.where(
                    occupied_ref[...] > 0, moved[low : low + cap], table[a, :, cols]
                )
                basis = moved[low + rows - 8 : low + rows]
                products += [basis * basis[k : k + 1] for k in range(1, COMPS + 1)]
            stored(n).start()
            products.append(jnp.zeros((256 - 24 * COMPS, SLICE), f32))
            weights = jnp.concatenate(products, axis=0).astype(bf16)
            damped = (jnp.concatenate([damping] * 3, axis=0) * (1.0 - bend * bend)).astype(bf16)
            damp_sum[...] += dot_nt(damped, weights)
            head = moved.astype(bf16)
            rest = (moved - head.astype(f32)).astype(bf16)
            load = loading_ref[:, cols]
            stress_sum[...] += dot_nt(head, load) + dot_nt(rest, load)

    def gathered(sums, shift):
        lanes = sums.shape[1]
        return (
            sums[0:rows]
            + pltpu.roll(sums[rows : 2 * rows], lanes - shift, 1)
            + pltpu.roll(sums[2 * rows : 3 * rows], lanes - 2 * shift, 1)
        )[:, 0:128]

    lane = lax.broadcasted_iota(jnp.int32, result_ref.shape, 1)
    stress = gathered(stress_sum[...], 8)
    damp = gathered(damp_sum[...], 8 * COMPS)
    result = jnp.where(lane < 8 * COMPS, damp, jnp.where(lane < 8 * COMPS + 8, stress, 0.0))
    result_ref[...] = result
    pick = pick_ref[...]
    head, middle, rest = three_parts(result)
    back_ref[...] = dot_nn(pick, head) + (dot_nn(pick, middle) + dot_nn(pick, rest))
    for n in range(BLOCKS):
        stored(n).wait()


def corner_kernel(own_ref, behind_ref, fixed_ref, own_data_ref, behind_data_ref, force_ref, block_ref, work, *, scale):
    lanes = work.shape[2]
    workers = own_ref.shape[0]
    total = jnp.zeros((16, NODE_DEV), f32)
    work[...] = jnp.zeros_like(work)
    for part, (arrived, data) in enumerate(((own_ref, own_data_ref), (behind_ref, behind_data_ref))):
        gx = data[0:1, :]
        gy = data[1:2, :]
        gz = data[2:3, :]
        volume = data[3:4, :] * scale
        node = data[4:5, :].astype(jnp.int32) - part * NODE_DEV
        worker = data[5:6, :].astype(jnp.int32)
        pick = (lax.broadcasted_iota(jnp.int32, (workers, lanes), 0) == worker).astype(f32)
        got = lax.dot_general(
            arrived[...], pick, (((0,), (0,)), ((), ())), preferred_element_type=f32, precision=highest
        )
        t = [fixed_ref[8 * j : 8 * j + 8, :] - got[8 * j : 8 * j + 8, :] for j in range(COMPS)]
        columns = (
            got[8 * COMPS : 8 * COMPS + 8, :],
            t[0] * gx + t[4] * gz + t[5] * gy,
            t[1] * gy + t[3] * gz + t[5] * gx,
            t[2] * gz + t[3] * gy + t[4] * gx,
        )
        for c, m in enumerate(columns):
            blocks = (
                m[1:2] * gx + m[5:6] * gz + m[6:7] * gy,
                m[2:3] * gy + m[4:5] * gz + m[6:7] * gx,
                m[3:4] * gz + m[4:5] * gy + m[5:6] * gx,
            )
            for a in range(3):
                r = a if c == 0 else 3 + 3 * a + c - 1
                work[part, r : r + 1, :] = blocks[a] * volume
        spread = (lax.broadcasted_iota(jnp.int32, (NODE_DEV, lanes), 0) == node).astype(f32)
        total += lax.dot_general(
            work[part], spread, (((1,), (1,)), ((), ())), preferred_element_type=f32, precision=highest
        )
    force_ref[...] = total[0:3]
    block_ref[...] = total[3:12]


def from_behind(block, axis, distance):
    devices = range(lax.axis_size(axis))
    route = [(i - distance, i) for i in devices if i - distance in devices]
    return lax.ppermute(block, axis, route)


RVE = ("z", "y", "core")
ALL = ("z", "y", "core", "blk")


def spread_network(compliance):
    rows, nodes = compliance.shape
    around = jnp.concatenate([compliance, compliance[:, : (SENT - 1) * SLICE]], axis=1)
    half = lax.dynamic_slice(around, (0, lax.axis_index("z") * SLICE), (rows, SENT * SLICE))
    count = lax.axis_size("y")
    line = lax.all_to_all(
        jnp.broadcast_to(half[None], (count,) + half.shape), "y", split_axis=0, concat_axis=0, tiled=True
    )
    plane = lax.all_gather(line.reshape(count * rows, SENT * SLICE), "z", axis=0, tiled=True)
    other = lax.ppermute(plane, "core", [(0, 1), (1, 0)])
    shape = (BLOCKS, count, rows, SENT * SLICE)
    return line, plane.reshape(shape), other.reshape(shape)


def body(
    strain, fiber_coeff, gradients, volume, corners, rve_worker, rve_slot, slot_element,
    state_table, loading, compliance,
):
    elems = strain.shape[0]
    workers = lax.axis_size(RVE)
    columns = lax.axis_size("blk")
    cap = state_table.shape[0]
    nodes = compliance.shape[1]
    rows = round_up(cap + COMPS, 8)

    line, mine, other = spread_network(compliance)

    worker_ids = jnp.arange(workers)
    send_pick = (worker_ids[:, None] == rve_worker[None, :]).astype(bf16)
    element_rows = jnp.concatenate([fiber_coeff, jnp.pad(strain, ((0, 0), (0, 128 - COMPS)))], axis=1)
    outgoing = jnp.dot(send_pick, element_rows)
    outgoing = lax.optimization_barrier((outgoing, line))[0]
    arrived = lax.all_to_all(outgoing, RVE, split_axis=0, concat_axis=0, tiled=True)

    device_rank = lax.axis_index(ALL)
    corner_data = jnp.concatenate(
        [
            jnp.transpose(gradients.reshape(4, 3, elems), (1, 0, 2)).reshape(3, 4 * elems),
            jnp.tile(volume, 4)[None, :],
            (corners - device_rank * NODE_DEV).reshape(1, 4 * elems).astype(f32),
            jnp.tile(rve_worker, 4)[None, :].astype(f32),
            jnp.zeros((2, 4 * elems), f32),
        ],
        axis=0,
    )
    behind_data = from_behind(corner_data, ALL, 1)

    occupied = slot_element >= 0
    home = jnp.where(occupied, slot_element // (elems * columns), -1)
    home_wide = jnp.pad(home, (0, rows - cap), constant_values=-1)
    slot_pick = (home_wide[:, None] == worker_ids[None, :]).astype(bf16)
    unit = (jnp.arange(rows)[:, None] - cap == jnp.arange(128)[None, :]).astype(f32)
    loading_rows = jnp.transpose(loading, (1, 0, 2))
    loading_wide = jnp.pad(loading_rows, ((0, 0), (0, 128 - COMPS), (0, 0)))
    loading_sums = jnp.pad(loading_rows, ((0, 0), (1, 1), (0, 0))).reshape(24, nodes)
    loading_sums = jnp.pad(loading_sums, ((8 * COMPS, 128 - 24 - 8 * COMPS), (0, 0)))
    states = jnp.transpose(state_table, (1, 0, 2))
    wide = nodes + (SENT - 1) * SLICE

    press, forcing, fiber = pl.pallas_call(
        prepare_kernel,
        out_shape=(
            jax.ShapeDtypeStruct((3 * rows, wide), bf16),
            jax.ShapeDtypeStruct((3, rows, nodes), f32),
            jax.ShapeDtypeStruct((rows, nodes), f32),
        ),
        scratch_shapes=[pltpu.VMEM((rows, SLICE), f32)],
        name="prepare",
    )(slot_pick, unit, arrived, loading_wide, states)

    vmem = pl.BlockSpec(memory_space=pltpu.VMEM)
    hbm = pl.BlockSpec(memory_space=pl.ANY)
    table, result, backward = pl.pallas_call(
        solve_kernel,
        out_shape=(
            jax.ShapeDtypeStruct((3, cap, nodes), f32),
            jax.ShapeDtypeStruct((rows, 128), f32),
            jax.ShapeDtypeStruct((workers, 128), f32),
        ),
        in_specs=[pl.BlockSpec(memory_space=pltpu.SMEM)] + [vmem] * 3 + [hbm] * 6,
        out_specs=(hbm, vmem, vmem),
        scratch_shapes=[
            pltpu.VMEM((BLOCKS, mine.shape[1], 2, mine.shape[2], SENT * SLICE), bf16),
            pltpu.VMEM((ITERS, 3 * rows, wide), bf16),
            pltpu.VMEM((3, rows, nodes), f32),
            pltpu.VMEM((rows, nodes), f32),
            pltpu.VMEM((3, cap, nodes), f32),
            pltpu.VMEM((3 * rows, 256), f32),
            pltpu.VMEM((3 * rows, 128), f32),
            pltpu.SemaphoreType.DMA((BLOCKS, 2)),
            pltpu.SemaphoreType.DMA((4,)),
            pltpu.SemaphoreType.DMA((BLOCKS,)),
        ],
        name="solve",
    )(
        lax.axis_index("core")[None].astype(jnp.int32), slot_pick.T, loading_sums,
        occupied.astype(jnp.int32)[:, None], press, forcing, fiber, states, mine, other,
    )
    new_table = jnp.transpose(table, (1, 0, 2))

    returned = lax.all_to_all(backward, RVE, split_axis=0, concat_axis=0, tiled=True)
    behind = from_behind(returned, ALL, 1)
    fixed = jnp.pad(result[cap : cap + COMPS, 8 * COMPS + 1 : 8 * COMPS + 1 + COMPS], ((0, 0), (1, 1)))
    forces, blocks = pl.pallas_call(
        functools.partial(corner_kernel, scale=1.0 / (3 * nodes)),
        out_shape=(
            jax.ShapeDtypeStruct((3, NODE_DEV), f32),
            jax.ShapeDtypeStruct((9, NODE_DEV), f32),
        ),
        scratch_shapes=[pltpu.VMEM((2, 16, 4 * elems), f32)],
        name="corners",
    )(returned, behind, fixed.reshape(8 * COMPS, 1), corner_data, behind_data)
    return (new_table, forces, blocks)


def solution(mesh):
    workers, columns = mesh.devices.shape
    mesh = jax.sharding.Mesh(mesh.devices.reshape(8, workers // 16, 2, columns), ALL)
    return jax.shard_map(
        body,
        mesh=mesh,
        in_specs=(
            P(ALL, None),
            P(ALL, None),
            P(None, ALL),
            P(ALL),
            P(None, ALL),
            P(ALL),
            P(ALL),
            P(ALL),
            P(ALL, None, None),
            P(),
            P(RVE, None),
        ),
        out_specs=(P(ALL, None, None), P(None, ALL), P(None, ALL)),
        check_vma=False,
    )
```

```python
import functools

import jax
import jax.numpy as jnp
from jax import lax
from jax.experimental import pallas as pl
from jax.experimental.pallas import tpu as pltpu
from jax.sharding import PartitionSpec as P

ITERS = 3
NODE_DEV = 128
COMPS = 6
SLICE = 256
BLOCKS = 8
SENT = 5

highest = lax.Precision.HIGHEST
f32 = jnp.float32
bf16 = jnp.bfloat16


def round_up(value, step):
    return (value + step - 1) // step * step


def dot_nn(left, right):
    return lax.dot_general(left, right, (((1,), (0,)), ((), ())), preferred_element_type=f32)


def dot_nt(left, right):
    return lax.dot_general(left, right, (((1,), (1,)), ((), ())), preferred_element_type=f32)


def three_parts(value):
    head = value.astype(bf16)
    rest = value - head.astype(f32)
    middle = rest.astype(bf16)
    return head, middle, (rest - middle.astype(f32)).astype(bf16)


def prepare_kernel(pick_ref, unit_ref, arrived_ref, loading_ref, state_ref, press_ref, forcing_ref, fiber_ref, still):
    cap = state_ref.shape[1]
    rows = pick_ref.shape[0]
    nodes = state_ref.shape[2]
    pick = pick_ref[...]
    strain = (dot_nn(pick, arrived_ref[:, nodes:]) + unit_ref[...]).astype(bf16)
    still[...] = jnp.zeros_like(still)
    for start in range(0, nodes, SLICE):
        cols = pl.ds(start, SLICE)
        fiber = dot_nn(pick, arrived_ref[:, cols])
        fiber_ref[:, cols] = fiber
        for a in range(3):
            still[0:cap, :] = state_ref[a, :, cols]
            forcing = dot_nn(strain, loading_ref[a, :, cols])
            forcing_ref[a, :, cols] = forcing
            first = (forcing - fiber * jnp.tanh(still[...])).astype(bf16)
            press_ref[a * rows : (a + 1) * rows, cols] = first
            if nodes + start < press_ref.shape[1]:
                press_ref[a * rows : (a + 1) * rows, pl.ds(nodes + start, SLICE)] = first


def solve_kernel(
    side_ref, pick_ref, loading_ref, occupied_ref, press_hbm, forcing_hbm, fiber_hbm, state_hbm,
    mine_hbm, other_hbm, table_hbm, result_ref, back_ref,
    network, pressure, forcing, fiber, table, damp_sum, stress_sum, net_sems, in_sems, out_sems,
):
    rows = fiber.shape[0]
    nodes = fiber.shape[1]
    cap = table.shape[1]

    def fetch(i, side, source, k):
        return pltpu.make_async_copy(source.at[i], network.at[i, :, side], net_sems.at[i, k])

    inputs = (
        pltpu.make_async_copy(press_hbm, pressure.at[0], in_sems.at[0]),
        pltpu.make_async_copy(forcing_hbm, forcing, in_sems.at[1]),
        pltpu.make_async_copy(fiber_hbm, fiber, in_sems.at[2]),
        pltpu.make_async_copy(state_hbm, table, in_sems.at[3]),
    )
    inputs[0].start()
    arrival = [(1 + i) % BLOCKS for i in range(BLOCKS)]
    for side in range(2):

        @pl.when(side_ref[0] == side)
        def _():
            for i in arrival:
                fetch(i, side, mine_hbm, 0).start()
                fetch(i, 1 - side, other_hbm, 1).start()

    for copy in inputs[1:]:
        copy.start()

    def wait_network(i):
        fetch(i, 0, mine_hbm, 0).wait()
        fetch(i, 0, other_hbm, 1).wait()

    def net(i, start, blocks):
        cols = pl.ds(start * SLICE, blocks * SLICE)
        return network[i, :, :, :, cols].reshape(SLICE, blocks * SLICE)

    def stored(n):
        return pltpu.make_async_copy(
            table.at[:, :, pl.ds(n * SLICE, SLICE)],
            table_hbm.at[:, :, pl.ds(n * SLICE, SLICE)],
            out_sems.at[n],
        )

    damp_sum[...] = jnp.zeros_like(damp_sum)
    stress_sum[...] = jnp.zeros_like(stress_sum)
    inputs[0].wait()
    for i in arrival[:3]:
        wait_network(i)
    for iteration in range(ITERS):
        source = pressure.at[iteration]
        for step in range(BLOCKS):
            n = (step + 4) % BLOCKS
            cols = pl.ds(n * SLICE, SLICE)
            if iteration == 0 and step < BLOCKS - 3:
                wait_network(n)
            moved = dot_nt(source[:, pl.ds(n * SLICE, SENT * SLICE)], net(n, 0, SENT))
            for d in range(1, BLOCKS - SENT + 1):
                i = (n - d) % BLOCKS
                moved += dot_nn(source[:, pl.ds(i * SLICE, SLICE)], net(i, d, 1))
            if iteration == 0 and step == 0:
                inputs[1].wait()
                inputs[2].wait()
            damping = fiber[:, cols]
            bend = jnp.tanh(moved)
            if iteration < ITERS - 1:
                for a in range(3):
                    block = slice(a * rows, (a + 1) * rows)
                    value = (forcing[a, :, cols] - damping * bend[block]).astype(bf16)
                    pressure[iteration + 1, block, cols] = value
                    if n < SENT - 1:
                        pressure[iteration + 1, block, pl.ds(nodes + n * SLICE, SLICE)] = value
                continue
            if step == 0:
                inputs[3].wait()
            products = []
            for a in range(3):
                low = a * rows
                table[a, :, cols] = jnp.where(
                    occupied_ref[...] > 0, moved[low : low + cap], table[a, :, cols]
                )
                basis = moved[low + rows - 8 : low + rows]
                products += [basis * basis[k : k + 1] for k in range(1, COMPS + 1)]
            stored(n).start()
            products.append(jnp.zeros((256 - 24 * COMPS, SLICE), f32))
            weights = jnp.concatenate(products, axis=0).astype(bf16)
            damped = (jnp.concatenate([damping] * 3, axis=0) * (1.0 - bend * bend)).astype(bf16)
            damp_sum[...] += dot_nt(damped, weights)
            head = moved.astype(bf16)
            rest = (moved - head.astype(f32)).astype(bf16)
            load = loading_ref[:, cols]
            stress_sum[...] += dot_nt(head, load) + dot_nt(rest, load)

    def gathered(sums, shift):
        lanes = sums.shape[1]
        return (
            sums[0:rows]
            + pltpu.roll(sums[rows : 2 * rows], lanes - shift, 1)
            + pltpu.roll(sums[2 * rows : 3 * rows], lanes - 2 * shift, 1)
        )[:, 0:128]

    lane = lax.broadcasted_iota(jnp.int32, result_ref.shape, 1)
    stress = gathered(stress_sum[...], 8)
    damp = gathered(damp_sum[...], 8 * COMPS)
    result = jnp.where(lane < 8 * COMPS, damp, jnp.where(lane < 8 * COMPS + 8, stress, 0.0))
    result_ref[...] = result
    pick = pick_ref[...]
    head, middle, rest = three_parts(result)
    back_ref[...] = dot_nn(pick, head) + (dot_nn(pick, middle) + dot_nn(pick, rest))
    for n in range(BLOCKS):
        stored(n).wait()


def corner_kernel(own_ref, behind_ref, fixed_ref, own_data_ref, behind_data_ref, force_ref, block_ref, work, *, scale):
    lanes = work.shape[2]
    workers = own_ref.shape[0]
    total = jnp.zeros((16, NODE_DEV), f32)
    work[...] = jnp.zeros_like(work)
    for part, (arrived, data) in enumerate(((own_ref, own_data_ref), (behind_ref, behind_data_ref))):
        gx = data[0:1, :]
        gy = data[1:2, :]
        gz = data[2:3, :]
        volume = data[3:4, :] * scale
        node = data[4:5, :].astype(jnp.int32) - part * NODE_DEV
        worker = data[5:6, :].astype(jnp.int32)
        pick = (lax.broadcasted_iota(jnp.int32, (workers, lanes), 0) == worker).astype(f32)
        got = lax.dot_general(
            arrived[...], pick, (((0,), (0,)), ((), ())), preferred_element_type=f32, precision=highest
        )
        t = [fixed_ref[8 * j : 8 * j + 8, :] - got[8 * j : 8 * j + 8, :] for j in range(COMPS)]
        columns = (
            got[8 * COMPS : 8 * COMPS + 8, :],
            t[0] * gx + t[4] * gz + t[5] * gy,
            t[1] * gy + t[3] * gz + t[5] * gx,
            t[2] * gz + t[3] * gy + t[4] * gx,
        )
        for c, m in enumerate(columns):
            blocks = (
                m[1:2] * gx + m[5:6] * gz + m[6:7] * gy,
                m[2:3] * gy + m[4:5] * gz + m[6:7] * gx,
                m[3:4] * gz + m[4:5] * gy + m[5:6] * gx,
            )
            for a in range(3):
                r = a if c == 0 else 3 + 3 * a + c - 1
                work[part, r : r + 1, :] = blocks[a] * volume
        spread = (lax.broadcasted_iota(jnp.int32, (NODE_DEV, lanes), 0) == node).astype(f32)
        total += lax.dot_general(
            work[part], spread, (((1,), (1,)), ((), ())), preferred_element_type=f32, precision=highest
        )
    force_ref[...] = total[0:3]
    block_ref[...] = total[3:12]


def from_behind(block, axis, distance):
    devices = range(lax.axis_size(axis))
    route = [(i - distance, i) for i in devices if i - distance in devices]
    return lax.ppermute(block, axis, route)


RVE = ("z", "y", "core")
ALL = ("z", "y", "core", "blk")


def spread_network(compliance):
    rows, nodes = compliance.shape
    around = jnp.concatenate([compliance, compliance[:, : (SENT - 1) * SLICE]], axis=1)
    half = lax.dynamic_slice(around, (0, lax.axis_index("z") * SLICE), (rows, SENT * SLICE))
    count = lax.axis_size("y")
    line = lax.all_to_all(
        jnp.broadcast_to(half[None], (count,) + half.shape), "y", split_axis=0, concat_axis=0, tiled=True
    )
    plane = lax.all_gather(line.reshape(count * rows, SENT * SLICE), "z", axis=0, tiled=True)
    return line, plane


def swap_cores(plane, rows):
    other = lax.ppermute(plane, "core", [(0, 1), (1, 0)])
    shape = (BLOCKS, plane.shape[0] // (BLOCKS * rows), rows, SENT * SLICE)
    return plane.reshape(shape), other.reshape(shape)


def body(
    strain, fiber_coeff, gradients, volume, corners, rve_worker, rve_slot, slot_element,
    state_table, loading, compliance,
):
    elems = strain.shape[0]
    workers = lax.axis_size(RVE)
    columns = lax.axis_size("blk")
    cap = state_table.shape[0]
    nodes = compliance.shape[1]
    rows = round_up(cap + COMPS, 8)

    line, plane = spread_network(compliance)

    worker_ids = jnp.arange(workers)
    send_pick = (worker_ids[:, None] == rve_worker[None, :]).astype(bf16)
    element_rows = jnp.concatenate([fiber_coeff, jnp.pad(strain, ((0, 0), (0, 128 - COMPS)))], axis=1)
    outgoing = jnp.dot(send_pick, element_rows)
    outgoing = lax.optimization_barrier((outgoing, line))[0]
    arrived = lax.all_to_all(outgoing, RVE, split_axis=0, concat_axis=0, tiled=True)

    device_rank = lax.axis_index(ALL)
    corner_data = jnp.concatenate(
        [
            jnp.transpose(gradients.reshape(4, 3, elems), (1, 0, 2)).reshape(3, 4 * elems),
            jnp.tile(volume, 4)[None, :],
            (corners - device_rank * NODE_DEV).reshape(1, 4 * elems).astype(f32),
            jnp.tile(rve_worker, 4)[None, :].astype(f32),
            jnp.zeros((2, 4 * elems), f32),
        ],
        axis=0,
    )
    behind_data = from_behind(corner_data, ALL, 1)

    occupied = slot_element >= 0
    home = jnp.where(occupied, slot_element // (elems * columns), -1)
    home_wide = jnp.pad(home, (0, rows - cap), constant_values=-1)
    slot_pick = (home_wide[:, None] == worker_ids[None, :]).astype(bf16)
    unit = (jnp.arange(rows)[:, None] - cap == jnp.arange(128)[None, :]).astype(f32)
    loading_rows = jnp.transpose(loading, (1, 0, 2))
    loading_wide = jnp.pad(loading_rows, ((0, 0), (0, 128 - COMPS), (0, 0)))
    loading_sums = jnp.pad(loading_rows, ((0, 0), (1, 1), (0, 0))).reshape(24, nodes)
    loading_sums = jnp.pad(loading_sums, ((8 * COMPS, 128 - 24 - 8 * COMPS), (0, 0)))
    states = jnp.transpose(state_table, (1, 0, 2))
    wide = nodes + (SENT - 1) * SLICE

    press, forcing, fiber = pl.pallas_call(
        prepare_kernel,
        out_shape=(
            jax.ShapeDtypeStruct((3 * rows, wide), bf16),
            jax.ShapeDtypeStruct((3, rows, nodes), f32),
            jax.ShapeDtypeStruct((rows, nodes), f32),
        ),
        scratch_shapes=[pltpu.VMEM((rows, SLICE), f32)],
        name="prepare",
    )(slot_pick, unit, arrived, loading_wide, states)
    plane, press, corner_data, behind_data, loading_sums, slot_give, occupied_rows = lax.optimization_barrier(
        (plane, press, corner_data, behind_data, loading_sums, slot_pick.T, occupied.astype(jnp.int32)[:, None])
    )
    mine, other = swap_cores(plane, compliance.shape[0])

    vmem = pl.BlockSpec(memory_space=pltpu.VMEM)
    hbm = pl.BlockSpec(memory_space=pl.ANY)
    table, result, backward = pl.pallas_call(
        solve_kernel,
        out_shape=(
            jax.ShapeDtypeStruct((3, cap, nodes), f32),
            jax.ShapeDtypeStruct((rows, 128), f32),
            jax.ShapeDtypeStruct((workers, 128), f32),
        ),
        in_specs=[pl.BlockSpec(memory_space=pltpu.SMEM)] + [vmem] * 3 + [hbm] * 6,
        out_specs=(hbm, vmem, vmem),
        scratch_shapes=[
            pltpu.VMEM((BLOCKS, mine.shape[1], 2, mine.shape[2], SENT * SLICE), bf16),
            pltpu.VMEM((ITERS, 3 * rows, wide), bf16),
            pltpu.VMEM((3, rows, nodes), f32),
            pltpu.VMEM((rows, nodes), f32),
            pltpu.VMEM((3, cap, nodes), f32),
            pltpu.VMEM((3 * rows, 256), f32),
            pltpu.VMEM((3 * rows, 128), f32),
            pltpu.SemaphoreType.DMA((BLOCKS, 2)),
            pltpu.SemaphoreType.DMA((4,)),
            pltpu.SemaphoreType.DMA((BLOCKS,)),
        ],
        name="solve",
    )(
        lax.axis_index("core")[None].astype(jnp.int32), slot_give, loading_sums,
        occupied_rows, press, forcing, fiber, states, mine, other,
    )
    new_table = jnp.transpose(table, (1, 0, 2))

    returned = lax.all_to_all(backward, RVE, split_axis=0, concat_axis=0, tiled=True)
    behind = from_behind(returned, ALL, 1)
    fixed = jnp.pad(result[cap : cap + COMPS, 8 * COMPS + 1 : 8 * COMPS + 1 + COMPS], ((0, 0), (1, 1)))
    forces, blocks = pl.pallas_call(
        functools.partial(corner_kernel, scale=1.0 / (3 * nodes)),
        out_shape=(
            jax.ShapeDtypeStruct((3, NODE_DEV), f32),
            jax.ShapeDtypeStruct((9, NODE_DEV), f32),
        ),
        scratch_shapes=[pltpu.VMEM((2, 16, 4 * elems), f32)],
        name="corners",
    )(returned, behind, fixed.reshape(8 * COMPS, 1), corner_data, behind_data)
    return (new_table, forces, blocks)


def solution(mesh):
    workers, columns = mesh.devices.shape
    mesh = jax.sharding.Mesh(mesh.devices.reshape(8, workers // 16, 2, columns), ALL)
    return jax.shard_map(
        body,
        mesh=mesh,
        in_specs=(
            P(ALL, None),
            P(ALL, None),
            P(None, ALL),
            P(ALL),
            P(None, ALL),
            P(ALL),
            P(ALL),
            P(ALL),
            P(ALL, None, None),
            P(),
            P(RVE, None),
        ),
        out_specs=(P(ALL, None, None), P(None, ALL), P(None, ALL)),
        check_vma=False,
    )
```

```python
import functools

import jax
import jax.numpy as jnp
from jax import lax
from jax.experimental import pallas as pl
from jax.experimental.pallas import tpu as pltpu
from jax.sharding import PartitionSpec as P

ITERS = 3
NODE_DEV = 128
COMPS = 6
SLICE = 256
BLOCKS = 8
SENT = 5
PARTS = 2

highest = lax.Precision.HIGHEST
f32 = jnp.float32
bf16 = jnp.bfloat16


def round_up(value, step):
    return (value + step - 1) // step * step


def dot_nn(left, right):
    return lax.dot_general(left, right, (((1,), (0,)), ((), ())), preferred_element_type=f32)


def dot_nt(left, right):
    return lax.dot_general(left, right, (((1,), (1,)), ((), ())), preferred_element_type=f32)


def three_parts(value):
    head = value.astype(bf16)
    rest = value - head.astype(f32)
    middle = rest.astype(bf16)
    return head, middle, (rest - middle.astype(f32)).astype(bf16)


def prepare_kernel(pick_ref, unit_ref, arrived_ref, loading_ref, state_ref, press_ref, forcing_ref, fiber_ref, still):
    cap = state_ref.shape[1]
    rows = pick_ref.shape[0]
    nodes = state_ref.shape[2]
    pick = pick_ref[...]
    strain = (dot_nn(pick, arrived_ref[:, nodes:]) + unit_ref[...]).astype(bf16)
    still[...] = jnp.zeros_like(still)
    for start in range(0, nodes, SLICE):
        cols = pl.ds(start, SLICE)
        fiber = dot_nn(pick, arrived_ref[:, cols])
        fiber_ref[:, cols] = fiber
        for a in range(3):
            still[0:cap, :] = state_ref[a, :, cols]
            forcing = dot_nn(strain, loading_ref[a, :, cols])
            forcing_ref[a, :, cols] = forcing
            first = (forcing - fiber * jnp.tanh(still[...])).astype(bf16)
            press_ref[a * rows : (a + 1) * rows, cols] = first
            if nodes + start < press_ref.shape[1]:
                press_ref[a * rows : (a + 1) * rows, pl.ds(nodes + start, SLICE)] = first


def solve_kernel(
    side_ref, pick_ref, loading_ref, occupied_ref, press_hbm, forcing_hbm, fiber_hbm, state_hbm, *refs,
):
    shares = refs[: 2 * PARTS]
    (
        table_hbm, result_ref, back_ref, network, pressure, forcing, fiber, table, damp_sum, stress_sum,
        net_sems, in_sems, out_sems,
    ) = refs[2 * PARTS :]
    rows = fiber.shape[0]
    nodes = fiber.shape[1]
    cap = table.shape[1]
    lines = network.shape[1] // PARTS

    def fetch(i, side, k):
        place = network.at[i, pl.ds(k % PARTS * lines, lines), side]
        return pltpu.make_async_copy(shares[k].at[i], place, net_sems.at[i, k])

    inputs = (
        pltpu.make_async_copy(press_hbm, pressure.at[0], in_sems.at[0]),
        pltpu.make_async_copy(forcing_hbm, forcing, in_sems.at[1]),
        pltpu.make_async_copy(fiber_hbm, fiber, in_sems.at[2]),
        pltpu.make_async_copy(state_hbm, table, in_sems.at[3]),
    )
    inputs[0].start()
    arrival = [(1 + i) % BLOCKS for i in range(BLOCKS)]
    for side in range(2):

        @pl.when(side_ref[0] == side)
        def _():
            for i in arrival:
                for k in range(2 * PARTS):
                    fetch(i, side if k < PARTS else 1 - side, k).start()

    for copy in inputs[1:]:
        copy.start()

    def wait_network(i):
        for k in range(2 * PARTS):
            fetch(i, 0, k).wait()

    def net(i, start, blocks):
        cols = pl.ds(start * SLICE, blocks * SLICE)
        return network[i, :, :, :, cols].reshape(SLICE, blocks * SLICE)

    def stored(n):
        return pltpu.make_async_copy(
            table.at[:, :, pl.ds(n * SLICE, SLICE)],
            table_hbm.at[:, :, pl.ds(n * SLICE, SLICE)],
            out_sems.at[n],
        )

    damp_sum[...] = jnp.zeros_like(damp_sum)
    stress_sum[...] = jnp.zeros_like(stress_sum)
    inputs[0].wait()
    for i in arrival[:3]:
        wait_network(i)
    for iteration in range(ITERS):
        source = pressure.at[iteration]
        for step in range(BLOCKS):
            n = (step + 4) % BLOCKS
            cols = pl.ds(n * SLICE, SLICE)
            if iteration == 0 and step < BLOCKS - 3:
                wait_network(n)
            moved = dot_nt(source[:, pl.ds(n * SLICE, SENT * SLICE)], net(n, 0, SENT))
            for d in range(1, BLOCKS - SENT + 1):
                i = (n - d) % BLOCKS
                moved += dot_nn(source[:, pl.ds(i * SLICE, SLICE)], net(i, d, 1))
            if iteration == 0 and step == 0:
                inputs[1].wait()
                inputs[2].wait()
            damping = fiber[:, cols]
            bend = jnp.tanh(moved)
            if iteration < ITERS - 1:
                for a in range(3):
                    block = slice(a * rows, (a + 1) * rows)
                    value = (forcing[a, :, cols] - damping * bend[block]).astype(bf16)
                    pressure[iteration + 1, block, cols] = value
                    if n < SENT - 1:
                        pressure[iteration + 1, block, pl.ds(nodes + n * SLICE, SLICE)] = value
                continue
            if step == 0:
                inputs[3].wait()
            products = []
            for a in range(3):
                low = a * rows
                table[a, :, cols] = jnp.where(
                    occupied_ref[...] > 0, moved[low : low + cap], table[a, :, cols]
                )
                basis = moved[low + rows - 8 : low + rows]
                products += [basis * basis[k : k + 1] for k in range(1, COMPS + 1)]
            stored(n).start()
            products.append(jnp.zeros((256 - 24 * COMPS, SLICE), f32))
            weights = jnp.concatenate(products, axis=0).astype(bf16)
            damped = (jnp.concatenate([damping] * 3, axis=0) * (1.0 - bend * bend)).astype(bf16)
            damp_sum[...] += dot_nt(damped, weights)
            head = moved.astype(bf16)
            rest = (moved - head.astype(f32)).astype(bf16)
            load = loading_ref[:, cols]
            stress_sum[...] += dot_nt(head, load) + dot_nt(rest, load)

    def gathered(sums, shift):
        lanes = sums.shape[1]
        return (
            sums[0:rows]
            + pltpu.roll(sums[rows : 2 * rows], lanes - shift, 1)
            + pltpu.roll(sums[2 * rows : 3 * rows], lanes - 2 * shift, 1)
        )[:, 0:128]

    lane = lax.broadcasted_iota(jnp.int32, result_ref.shape, 1)
    stress = gathered(stress_sum[...], 8)
    damp = gathered(damp_sum[...], 8 * COMPS)
    result = jnp.where(lane < 8 * COMPS, damp, jnp.where(lane < 8 * COMPS + 8, stress, 0.0))
    result_ref[...] = result
    pick = pick_ref[...]
    head, middle, rest = three_parts(result)
    back_ref[...] = dot_nn(pick, head) + (dot_nn(pick, middle) + dot_nn(pick, rest))
    for n in range(BLOCKS):
        stored(n).wait()


def corner_kernel(own_ref, behind_ref, fixed_ref, own_data_ref, behind_data_ref, force_ref, block_ref, work, *, scale):
    lanes = work.shape[2]
    workers = own_ref.shape[0]
    total = jnp.zeros((16, NODE_DEV), f32)
    work[...] = jnp.zeros_like(work)
    for part, (arrived, data) in enumerate(((own_ref, own_data_ref), (behind_ref, behind_data_ref))):
        gx = data[0:1, :]
        gy = data[1:2, :]
        gz = data[2:3, :]
        volume = data[3:4, :] * scale
        node = data[4:5, :].astype(jnp.int32) - part * NODE_DEV
        worker = data[5:6, :].astype(jnp.int32)
        pick = (lax.broadcasted_iota(jnp.int32, (workers, lanes), 0) == worker).astype(f32)
        got = lax.dot_general(
            arrived[...], pick, (((0,), (0,)), ((), ())), preferred_element_type=f32, precision=highest
        )
        t = [fixed_ref[8 * j : 8 * j + 8, :] - got[8 * j : 8 * j + 8, :] for j in range(COMPS)]
        columns = (
            got[8 * COMPS : 8 * COMPS + 8, :],
            t[0] * gx + t[4] * gz + t[5] * gy,
            t[1] * gy + t[3] * gz + t[5] * gx,
            t[2] * gz + t[3] * gy + t[4] * gx,
        )
        for c, m in enumerate(columns):
            blocks = (
                m[1:2] * gx + m[5:6] * gz + m[6:7] * gy,
                m[2:3] * gy + m[4:5] * gz + m[6:7] * gx,
                m[3:4] * gz + m[4:5] * gy + m[5:6] * gx,
            )
            for a in range(3):
                r = a if c == 0 else 3 + 3 * a + c - 1
                work[part, r : r + 1, :] = blocks[a] * volume
        spread = (lax.broadcasted_iota(jnp.int32, (NODE_DEV, lanes), 0) == node).astype(f32)
        total += lax.dot_general(
            work[part], spread, (((1,), (1,)), ((), ())), preferred_element_type=f32, precision=highest
        )
    force_ref[...] = total[0:3]
    block_ref[...] = total[3:12]


def from_behind(block, axis, distance):
    devices = range(lax.axis_size(axis))
    route = [(i - distance, i) for i in devices if i - distance in devices]
    return lax.ppermute(block, axis, route)


RVE = ("z", "y", "core")
ALL = ("z", "y", "core", "blk")


def spread_network(compliance):
    rows, nodes = compliance.shape
    around = jnp.concatenate([compliance, compliance[:, : (SENT - 1) * SLICE]], axis=1)
    half = lax.dynamic_slice(around, (0, lax.axis_index("z") * SLICE), (rows, SENT * SLICE))
    count = lax.axis_size("y")
    line = lax.all_to_all(
        jnp.broadcast_to(half[None], (count,) + half.shape), "y", split_axis=0, concat_axis=0, tiled=True
    )
    line = line.reshape(count * rows, SENT * SLICE)
    part = count * rows // PARTS
    planes = [
        lax.all_gather(line[p * part : (p + 1) * part], "z", axis=0, tiled=True) for p in range(PARTS)
    ]
    return line, planes


def swap_cores(planes, rows):
    others = [lax.ppermute(plane, "core", [(0, 1), (1, 0)]) for plane in planes]
    shape = (BLOCKS, planes[0].shape[0] // (BLOCKS * rows), rows, SENT * SLICE)
    return [block.reshape(shape) for block in planes + others]


def body(
    strain, fiber_coeff, gradients, volume, corners, rve_worker, rve_slot, slot_element,
    state_table, loading, compliance,
):
    elems = strain.shape[0]
    workers = lax.axis_size(RVE)
    columns = lax.axis_size("blk")
    cap = state_table.shape[0]
    nodes = compliance.shape[1]
    rows = round_up(cap + COMPS, 8)

    line, planes = spread_network(compliance)

    worker_ids = jnp.arange(workers)
    send_pick = (worker_ids[:, None] == rve_worker[None, :]).astype(bf16)
    element_rows = jnp.concatenate([fiber_coeff, jnp.pad(strain, ((0, 0), (0, 128 - COMPS)))], axis=1)
    outgoing = jnp.dot(send_pick, element_rows)
    outgoing = lax.optimization_barrier((outgoing, line))[0]
    arrived = lax.all_to_all(outgoing, RVE, split_axis=0, concat_axis=0, tiled=True)

    occupied = slot_element >= 0
    home = jnp.where(occupied, slot_element // (elems * columns), -1)
    home_wide = jnp.pad(home, (0, rows - cap), constant_values=-1)
    slot_pick = (home_wide[:, None] == worker_ids[None, :]).astype(bf16)
    unit = (jnp.arange(rows)[:, None] - cap == jnp.arange(128)[None, :]).astype(f32)
    loading_rows = jnp.transpose(loading, (1, 0, 2))
    loading_wide = jnp.pad(loading_rows, ((0, 0), (0, 128 - COMPS), (0, 0)))
    loading_sums = jnp.pad(loading_rows, ((0, 0), (1, 1), (0, 0))).reshape(24, nodes)
    loading_sums = jnp.pad(loading_sums, ((8 * COMPS, 128 - 24 - 8 * COMPS), (0, 0)))
    states = jnp.transpose(state_table, (1, 0, 2))
    wide = nodes + (SENT - 1) * SLICE

    press, forcing, fiber = pl.pallas_call(
        prepare_kernel,
        out_shape=(
            jax.ShapeDtypeStruct((3 * rows, wide), bf16),
            jax.ShapeDtypeStruct((3, rows, nodes), f32),
            jax.ShapeDtypeStruct((rows, nodes), f32),
        ),
        scratch_shapes=[pltpu.VMEM((rows, SLICE), f32)],
        name="prepare",
    )(slot_pick, unit, arrived, loading_wide, states)
    gradients, volume, corners, rve_worker = lax.optimization_barrier(
        (press, gradients, volume, corners, rve_worker)
    )[1:]
    device_rank = lax.axis_index(ALL)
    corner_data = jnp.concatenate(
        [
            jnp.transpose(gradients.reshape(4, 3, elems), (1, 0, 2)).reshape(3, 4 * elems),
            jnp.tile(volume, 4)[None, :],
            (corners - device_rank * NODE_DEV).reshape(1, 4 * elems).astype(f32),
            jnp.tile(rve_worker, 4)[None, :].astype(f32),
            jnp.zeros((2, 4 * elems), f32),
        ],
        axis=0,
    )
    behind_data = from_behind(corner_data, ALL, 1)

    planes, press, corner_data, behind_data, loading_sums, slot_give, occupied_rows = lax.optimization_barrier(
        (planes, press, corner_data, behind_data, loading_sums, slot_pick.T, occupied.astype(jnp.int32)[:, None])
    )
    shares = swap_cores(planes, compliance.shape[0])

    vmem = pl.BlockSpec(memory_space=pltpu.VMEM)
    hbm = pl.BlockSpec(memory_space=pltpu.HBM)
    table, result, backward = pl.pallas_call(
        solve_kernel,
        out_shape=(
            jax.ShapeDtypeStruct((3, cap, nodes), f32),
            jax.ShapeDtypeStruct((rows, 128), f32),
            jax.ShapeDtypeStruct((workers, 128), f32),
        ),
        in_specs=[pl.BlockSpec(memory_space=pltpu.SMEM)] + [vmem] * 3 + [hbm] * (4 + 2 * PARTS),
        out_specs=(hbm, vmem, vmem),
        scratch_shapes=[
            pltpu.VMEM((BLOCKS, PARTS * shares[0].shape[1], 2, shares[0].shape[2], SENT * SLICE), bf16),
            pltpu.VMEM((ITERS, 3 * rows, wide), bf16),
            pltpu.VMEM((3, rows, nodes), f32),
            pltpu.VMEM((rows, nodes), f32),
            pltpu.VMEM((3, cap, nodes), f32),
            pltpu.VMEM((3 * rows, 256), f32),
            pltpu.VMEM((3 * rows, 128), f32),
            pltpu.SemaphoreType.DMA((BLOCKS, 2 * PARTS)),
            pltpu.SemaphoreType.DMA((4,)),
            pltpu.SemaphoreType.DMA((BLOCKS,)),
        ],
        name="solve",
    )(
        lax.axis_index("core")[None].astype(jnp.int32), slot_give, loading_sums,
        occupied_rows, press, forcing, fiber, states, *shares,
    )
    new_table = jnp.transpose(table, (1, 0, 2))

    returned = lax.all_to_all(backward, RVE, split_axis=0, concat_axis=0, tiled=True)
    fixed = jnp.pad(result[cap : cap + COMPS, 8 * COMPS + 1 : 8 * COMPS + 1 + COMPS], ((0, 0), (1, 1)))
    fixed, returned = lax.optimization_barrier((fixed.reshape(8 * COMPS, 1), returned))
    behind = from_behind(returned, ALL, 1)
    forces, blocks = pl.pallas_call(
        functools.partial(corner_kernel, scale=1.0 / (3 * nodes)),
        out_shape=(
            jax.ShapeDtypeStruct((3, NODE_DEV), f32),
            jax.ShapeDtypeStruct((9, NODE_DEV), f32),
        ),
        scratch_shapes=[pltpu.VMEM((2, 16, 4 * elems), f32)],
        compiler_params=pltpu.CompilerParams(vmem_limit_bytes=8 << 20),
        name="corners",
    )(returned, behind, fixed, corner_data, behind_data)
    return (new_table, forces, blocks)


def solution(mesh):
    workers, columns = mesh.devices.shape
    mesh = jax.sharding.Mesh(mesh.devices.reshape(8, workers // 16, 2, columns), ALL)
    return jax.shard_map(
        body,
        mesh=mesh,
        in_specs=(
            P(ALL, None),
            P(ALL, None),
            P(None, ALL),
            P(ALL),
            P(None, ALL),
            P(ALL),
            P(ALL),
            P(ALL),
            P(ALL, None, None),
            P(),
            P(RVE, None),
        ),
        out_specs=(P(ALL, None, None), P(None, ALL), P(None, ALL)),
        check_vma=False,
    )
```

```python
import functools

import jax
import jax.numpy as jnp
from jax import lax
from jax.experimental import pallas as pl
from jax.experimental.pallas import tpu as pltpu
from jax.sharding import PartitionSpec as P

ITERS = 3
NODE_DEV = 128
COMPS = 6
SLICE = 256
BLOCKS = 8
SENT = 5
PIECES = 5

highest = lax.Precision.HIGHEST
f32 = jnp.float32
bf16 = jnp.bfloat16


def round_up(value, step):
    return (value + step - 1) // step * step


def dot_nn(left, right):
    return lax.dot_general(left, right, (((1,), (0,)), ((), ())), preferred_element_type=f32)


def dot_nt(left, right):
    return lax.dot_general(left, right, (((1,), (1,)), ((), ())), preferred_element_type=f32)


def three_parts(value):
    head = value.astype(bf16)
    rest = value - head.astype(f32)
    middle = rest.astype(bf16)
    return head, middle, (rest - middle.astype(f32)).astype(bf16)


def prepare_kernel(pick_ref, unit_ref, arrived_ref, loading_ref, state_ref, press_ref, forcing_ref, fiber_ref, still):
    cap = state_ref.shape[1]
    rows = pick_ref.shape[0]
    nodes = state_ref.shape[2]
    pick = pick_ref[...]
    strain = (dot_nn(pick, arrived_ref[:, nodes:]) + unit_ref[...]).astype(bf16)
    still[...] = jnp.zeros_like(still)
    for start in range(0, nodes, SLICE):
        cols = pl.ds(start, SLICE)
        fiber = dot_nn(pick, arrived_ref[:, cols])
        fiber_ref[:, cols] = fiber
        for a in range(3):
            still[0:cap, :] = state_ref[a, :, cols]
            forcing = dot_nn(strain, loading_ref[a, :, cols])
            forcing_ref[a, :, cols] = forcing
            first = (forcing - fiber * jnp.tanh(still[...])).astype(bf16)
            press_ref[a * rows : (a + 1) * rows, cols] = first
            if nodes + start < press_ref.shape[1]:
                press_ref[a * rows : (a + 1) * rows, pl.ds(nodes + start, SLICE)] = first


def solve_kernel(
    side_ref, pick_ref, loading_ref, occupied_ref, press_hbm, forcing_hbm, fiber_hbm, state_hbm, *refs,
):
    shares = refs[: 2 * PIECES]
    (
        table_hbm, result_ref, back_ref, network, pressure, forcing, fiber, table, damp_sum, stress_sum,
        net_sems, in_sems, out_sems,
    ) = refs[2 * PIECES :]
    rows = fiber.shape[0]
    nodes = fiber.shape[1]
    cap = table.shape[1]
    half_rows = network.shape[3] // 2
    width = network.shape[4] // 2

    def fetch(k):
        depth = shares[k].shape[0]
        turn = (0, 3, 1, 2, 2)[k % PIECES]
        side = side_ref[0] if k < PIECES else 1 - side_ref[0]
        quarter = (side_ref[1] + turn) % 4
        place = network.at[
            pl.ds(BLOCKS // 2 if k % PIECES == PIECES - 1 else 0, depth), :, side,
            pl.ds(pl.multiple_of(quarter // 2 * half_rows, half_rows), half_rows),
            pl.ds(pl.multiple_of(quarter % 2 * width, width), width),
        ]
        return pltpu.make_async_copy(shares[k], place, net_sems.at[k])

    inputs = (
        pltpu.make_async_copy(press_hbm, pressure.at[0], in_sems.at[0]),
        pltpu.make_async_copy(forcing_hbm, forcing, in_sems.at[1]),
        pltpu.make_async_copy(fiber_hbm, fiber, in_sems.at[2]),
        pltpu.make_async_copy(state_hbm, table, in_sems.at[3]),
    )
    inputs[0].start()
    for k in range(2 * PIECES):
        fetch(k).start()
    for copy in inputs[1:]:
        copy.start()

    def net(i, start, blocks):
        cols = pl.ds(start * SLICE, blocks * SLICE)
        return network[i, :, :, :, cols].reshape(SLICE, blocks * SLICE)

    def stored(n):
        return pltpu.make_async_copy(
            table.at[:, :, pl.ds(n * SLICE, SLICE)],
            table_hbm.at[:, :, pl.ds(n * SLICE, SLICE)],
            out_sems.at[n],
        )

    damp_sum[...] = jnp.zeros_like(damp_sum)
    stress_sum[...] = jnp.zeros_like(stress_sum)
    inputs[0].wait()
    for k in range(2 * PIECES):
        fetch(k).wait()
    for iteration in range(ITERS):
        source = pressure.at[iteration]
        for step in range(BLOCKS):
            n = step
            cols = pl.ds(n * SLICE, SLICE)
            moved = dot_nt(source[:, pl.ds(n * SLICE, SENT * SLICE)], net(n, 0, SENT))
            for d in range(1, BLOCKS - SENT + 1):
                i = (n - d) % BLOCKS
                moved += dot_nn(source[:, pl.ds(i * SLICE, SLICE)], net(i, d, 1))
            if iteration == 0 and step == 0:
                inputs[1].wait()
                inputs[2].wait()
            damping = fiber[:, cols]
            bend = jnp.tanh(moved)
            if iteration < ITERS - 1:
                for a in range(3):
                    block = slice(a * rows, (a + 1) * rows)
                    value = (forcing[a, :, cols] - damping * bend[block]).astype(bf16)
                    pressure[iteration + 1, block, cols] = value
                    if n < SENT - 1:
                        pressure[iteration + 1, block, pl.ds(nodes + n * SLICE, SLICE)] = value
                continue
            if step == 0:
                inputs[3].wait()
            products = []
            for a in range(3):
                low = a * rows
                table[a, :, cols] = jnp.where(
                    occupied_ref[...] > 0, moved[low : low + cap], table[a, :, cols]
                )
                basis = moved[low + rows - 8 : low + rows]
                products += [basis * basis[k : k + 1] for k in range(1, COMPS + 1)]
            stored(n).start()
            products.append(jnp.zeros((256 - 24 * COMPS, SLICE), f32))
            weights = jnp.concatenate(products, axis=0).astype(bf16)
            damped = (jnp.concatenate([damping] * 3, axis=0) * (1.0 - bend * bend)).astype(bf16)
            damp_sum[...] += dot_nt(damped, weights)
            head = moved.astype(bf16)
            rest = (moved - head.astype(f32)).astype(bf16)
            load = loading_ref[:, cols]
            stress_sum[...] += dot_nt(head, load) + dot_nt(rest, load)

    def gathered(sums, shift):
        lanes = sums.shape[1]
        return (
            sums[0:rows]
            + pltpu.roll(sums[rows : 2 * rows], lanes - shift, 1)
            + pltpu.roll(sums[2 * rows : 3 * rows], lanes - 2 * shift, 1)
        )[:, 0:128]

    lane = lax.broadcasted_iota(jnp.int32, result_ref.shape, 1)
    stress = gathered(stress_sum[...], 8)
    damp = gathered(damp_sum[...], 8 * COMPS)
    result = jnp.where(lane < 8 * COMPS, damp, jnp.where(lane < 8 * COMPS + 8, stress, 0.0))
    result_ref[...] = result
    pick = pick_ref[...]
    head, middle, rest = three_parts(result)
    back_ref[...] = dot_nn(pick, head) + (dot_nn(pick, middle) + dot_nn(pick, rest))
    for n in range(BLOCKS):
        stored(n).wait()


def corner_kernel(own_ref, behind_ref, fixed_ref, own_data_ref, behind_data_ref, force_ref, block_ref, work, *, scale):
    lanes = work.shape[2]
    workers = own_ref.shape[0]
    total = jnp.zeros((16, NODE_DEV), f32)
    work[...] = jnp.zeros_like(work)
    for part, (arrived, data) in enumerate(((own_ref, own_data_ref), (behind_ref, behind_data_ref))):
        gx = data[0:1, :]
        gy = data[1:2, :]
        gz = data[2:3, :]
        volume = data[3:4, :] * scale
        node = data[4:5, :].astype(jnp.int32) - part * NODE_DEV
        worker = data[5:6, :].astype(jnp.int32)
        pick = (lax.broadcasted_iota(jnp.int32, (workers, lanes), 0) == worker).astype(f32)
        got = lax.dot_general(
            arrived[...], pick, (((0,), (0,)), ((), ())), preferred_element_type=f32, precision=highest
        )
        t = [fixed_ref[8 * j : 8 * j + 8, :] - got[8 * j : 8 * j + 8, :] for j in range(COMPS)]
        columns = (
            got[8 * COMPS : 8 * COMPS + 8, :],
            t[0] * gx + t[4] * gz + t[5] * gy,
            t[1] * gy + t[3] * gz + t[5] * gx,
            t[2] * gz + t[3] * gy + t[4] * gx,
        )
        for c, m in enumerate(columns):
            blocks = (
                m[1:2] * gx + m[5:6] * gz + m[6:7] * gy,
                m[2:3] * gy + m[4:5] * gz + m[6:7] * gx,
                m[3:4] * gz + m[4:5] * gy + m[5:6] * gx,
            )
            for a in range(3):
                r = a if c == 0 else 3 + 3 * a + c - 1
                work[part, r : r + 1, :] = blocks[a] * volume
        spread = (lax.broadcasted_iota(jnp.int32, (NODE_DEV, lanes), 0) == node).astype(f32)
        total += lax.dot_general(
            work[part], spread, (((1,), (1,)), ((), ())), preferred_element_type=f32, precision=highest
        )
    force_ref[...] = total[0:3]
    block_ref[...] = total[3:12]


def from_behind(block, axis, distance):
    devices = range(lax.axis_size(axis))
    route = [(i - distance, i) for i in devices if i - distance in devices]
    return lax.ppermute(block, axis, route)


RVE = ("z", "y", "core")
ALL = ("z", "y", "core", "blk")


def spread_network(compliance):
    rows, nodes = compliance.shape
    ring = lax.axis_size("blk")
    width = SENT * SLICE // 2
    around = jnp.concatenate([compliance, compliance[:, : (SENT - 1) * SLICE]], axis=1)
    quarter = lax.axis_index("blk")
    start = (quarter // 2 * (rows // 2), lax.axis_index("z") * SLICE + quarter % 2 * width)
    part = lax.dynamic_slice(around, start, (rows // 2, width))
    depth, lines = lax.axis_size("z"), lax.axis_size("y")
    own = lax.all_to_all(
        jnp.broadcast_to(part[None], (depth * lines,) + part.shape), ("z", "y"),
        split_axis=0, concat_axis=0, tiled=True,
    ).reshape((depth, lines) + part.shape)

    def pass_on(value, step):
        return lax.ppermute(value, "blk", [(i, (i + step) % ring) for i in range(ring)])

    before = pass_on(own, 1)
    after = pass_on(own, -1)
    across = [pass_on(before[: depth // 2], 1), pass_on(after[depth // 2 :], -1)]
    pieces = [own, before, after] + across
    return own, pieces + [lax.ppermute(piece, "core", [(0, 1), (1, 0)]) for piece in pieces]


def body(
    strain, fiber_coeff, gradients, volume, corners, rve_worker, rve_slot, slot_element,
    state_table, loading, compliance,
):
    elems = strain.shape[0]
    workers = lax.axis_size(RVE)
    columns = lax.axis_size("blk")
    cap = state_table.shape[0]
    nodes = compliance.shape[1]
    rows = round_up(cap + COMPS, 8)

    own, shares = spread_network(compliance)

    worker_ids = jnp.arange(workers)
    send_pick = (worker_ids[:, None] == rve_worker[None, :]).astype(bf16)
    element_rows = jnp.concatenate([fiber_coeff, jnp.pad(strain, ((0, 0), (0, 128 - COMPS)))], axis=1)
    outgoing = jnp.dot(send_pick, element_rows)
    outgoing = lax.optimization_barrier((outgoing, own))[0]
    arrived = lax.all_to_all(outgoing, RVE, split_axis=0, concat_axis=0, tiled=True)

    occupied = slot_element >= 0
    home = jnp.where(occupied, slot_element // (elems * columns), -1)
    home_wide = jnp.pad(home, (0, rows - cap), constant_values=-1)
    slot_pick = (home_wide[:, None] == worker_ids[None, :]).astype(bf16)
    unit = (jnp.arange(rows)[:, None] - cap == jnp.arange(128)[None, :]).astype(f32)
    loading_rows = jnp.transpose(loading, (1, 0, 2))
    loading_wide = jnp.pad(loading_rows, ((0, 0), (0, 128 - COMPS), (0, 0)))
    loading_sums = jnp.pad(loading_rows, ((0, 0), (1, 1), (0, 0))).reshape(24, nodes)
    loading_sums = jnp.pad(loading_sums, ((8 * COMPS, 128 - 24 - 8 * COMPS), (0, 0)))
    states = jnp.transpose(state_table, (1, 0, 2))
    wide = nodes + (SENT - 1) * SLICE

    press, forcing, fiber = pl.pallas_call(
        prepare_kernel,
        out_shape=(
            jax.ShapeDtypeStruct((3 * rows, wide), bf16),
            jax.ShapeDtypeStruct((3, rows, nodes), f32),
            jax.ShapeDtypeStruct((rows, nodes), f32),
        ),
        scratch_shapes=[pltpu.VMEM((rows, SLICE), f32)],
        name="prepare",
    )(slot_pick, unit, arrived, loading_wide, states)
    gradients, volume, corners, rve_worker = lax.optimization_barrier(
        (press, gradients, volume, corners, rve_worker)
    )[1:]
    device_rank = lax.axis_index(ALL)
    corner_data = jnp.concatenate(
        [
            jnp.transpose(gradients.reshape(4, 3, elems), (1, 0, 2)).reshape(3, 4 * elems),
            jnp.tile(volume, 4)[None, :],
            (corners - device_rank * NODE_DEV).reshape(1, 4 * elems).astype(f32),
            jnp.tile(rve_worker, 4)[None, :].astype(f32),
            jnp.zeros((2, 4 * elems), f32),
        ],
        axis=0,
    )
    behind_data = from_behind(corner_data, ALL, 1)

    press, corner_data, behind_data, loading_sums, slot_give, occupied_rows = lax.optimization_barrier(
        (press, corner_data, behind_data, loading_sums, slot_pick.T, occupied.astype(jnp.int32)[:, None])
    )

    vmem = pl.BlockSpec(memory_space=pltpu.VMEM)
    hbm = pl.BlockSpec(memory_space=pltpu.HBM)
    table, result, backward = pl.pallas_call(
        solve_kernel,
        out_shape=(
            jax.ShapeDtypeStruct((3, cap, nodes), f32),
            jax.ShapeDtypeStruct((rows, 128), f32),
            jax.ShapeDtypeStruct((workers, 128), f32),
        ),
        in_specs=[pl.BlockSpec(memory_space=pltpu.SMEM)] + [vmem] * 3 + [hbm] * (4 + 2 * PIECES),
        out_specs=(hbm, vmem, vmem),
        scratch_shapes=[
            pltpu.VMEM((BLOCKS, lax.axis_size("y"), 2, compliance.shape[0], SENT * SLICE), bf16),
            pltpu.VMEM((ITERS, 3 * rows, wide), bf16),
            pltpu.VMEM((3, rows, nodes), f32),
            pltpu.VMEM((rows, nodes), f32),
            pltpu.VMEM((3, cap, nodes), f32),
            pltpu.VMEM((3 * rows, 256), f32),
            pltpu.VMEM((3 * rows, 128), f32),
            pltpu.SemaphoreType.DMA((2 * PIECES,)),
            pltpu.SemaphoreType.DMA((4,)),
            pltpu.SemaphoreType.DMA((BLOCKS,)),
        ],
        name="solve",
    )(
        jnp.stack([lax.axis_index("core"), lax.axis_index("blk")]).astype(jnp.int32), slot_give, loading_sums,
        occupied_rows, press, forcing, fiber, states, *shares,
    )
    new_table = jnp.transpose(table, (1, 0, 2))

    returned = lax.all_to_all(backward, RVE, split_axis=0, concat_axis=0, tiled=True)
    fixed = jnp.pad(result[cap : cap + COMPS, 8 * COMPS + 1 : 8 * COMPS + 1 + COMPS], ((0, 0), (1, 1)))
    fixed, returned = lax.optimization_barrier((fixed.reshape(8 * COMPS, 1), returned))
    behind = from_behind(returned, ALL, 1)
    forces, blocks = pl.pallas_call(
        functools.partial(corner_kernel, scale=1.0 / (3 * nodes)),
        out_shape=(
            jax.ShapeDtypeStruct((3, NODE_DEV), f32),
            jax.ShapeDtypeStruct((9, NODE_DEV), f32),
        ),
        scratch_shapes=[pltpu.VMEM((2, 16, 4 * elems), f32)],
        compiler_params=pltpu.CompilerParams(vmem_limit_bytes=8 << 20),
        name="corners",
    )(returned, behind, fixed, corner_data, behind_data)
    return (new_table, forces, blocks)


def solution(mesh):
    workers, columns = mesh.devices.shape
    mesh = jax.sharding.Mesh(mesh.devices.reshape(8, workers // 16, 2, columns), ALL)
    return jax.shard_map(
        body,
        mesh=mesh,
        in_specs=(
            P(ALL, None),
            P(ALL, None),
            P(None, ALL),
            P(ALL),
            P(None, ALL),
            P(ALL),
            P(ALL),
            P(ALL),
            P(ALL, None, None),
            P(),
            P(RVE, None),
        ),
        out_specs=(P(ALL, None, None), P(None, ALL), P(None, ALL)),
        check_vma=False,
    )
```

```python
import functools

import jax
import jax.numpy as jnp
from jax import lax
from jax.experimental import pallas as pl
from jax.experimental.pallas import tpu as pltpu
from jax.sharding import PartitionSpec as P

ITERS = 3
NODE_DEV = 128
COMPS = 6
SLICE = 256
BLOCKS = 8
SENT = 5
PIECES = ((0, 0), (3, 0), (3, 1), (1, 0), (1, 1), (2, 0), (2, 1))

highest = lax.Precision.HIGHEST
f32 = jnp.float32
bf16 = jnp.bfloat16


def round_up(value, step):
    return (value + step - 1) // step * step


def dot_nn(left, right):
    return lax.dot_general(left, right, (((1,), (0,)), ((), ())), preferred_element_type=f32)


def dot_nt(left, right):
    return lax.dot_general(left, right, (((1,), (1,)), ((), ())), preferred_element_type=f32)


def three_parts(value):
    head = value.astype(bf16)
    rest = value - head.astype(f32)
    middle = rest.astype(bf16)
    return head, middle, (rest - middle.astype(f32)).astype(bf16)


def prepare_kernel(pick_ref, unit_ref, arrived_ref, loading_ref, state_ref, press_ref, forcing_ref, fiber_ref, still):
    cap = state_ref.shape[1]
    rows = pick_ref.shape[0]
    nodes = state_ref.shape[2]
    pick = pick_ref[...]
    strain = (dot_nn(pick, arrived_ref[:, nodes:]) + unit_ref[...]).astype(bf16)
    still[...] = jnp.zeros_like(still)
    for start in range(0, nodes, SLICE):
        cols = pl.ds(start, SLICE)
        fiber = dot_nn(pick, arrived_ref[:, cols])
        fiber_ref[:, cols] = fiber
        for a in range(3):
            still[0:cap, :] = state_ref[a, :, cols]
            forcing = dot_nn(strain, loading_ref[a, :, cols])
            forcing_ref[a, :, cols] = forcing
            first = (forcing - fiber * jnp.tanh(still[...])).astype(bf16)
            press_ref[a * rows : (a + 1) * rows, cols] = first
            if nodes + start < press_ref.shape[1]:
                press_ref[a * rows : (a + 1) * rows, pl.ds(nodes + start, SLICE)] = first


def solve_kernel(
    side_ref, pick_ref, loading_ref, occupied_ref, press_hbm, forcing_hbm, fiber_hbm, state_hbm, *refs,
):
    shares = refs[: 2 * len(PIECES)]
    (
        table_hbm, result_ref, back_ref, network, pressure, forcing, fiber, table, damp_sum, stress_sum,
        net_sems, in_sems, out_sems,
    ) = refs[2 * len(PIECES) :]
    rows = fiber.shape[0]
    nodes = fiber.shape[1]
    cap = table.shape[1]
    half_rows = network.shape[3] // 2
    width = network.shape[4] // 2

    def fetch(k):
        depth = shares[k].shape[0]
        turn, late = PIECES[k % len(PIECES)]
        side = side_ref[0] if k < len(PIECES) else 1 - side_ref[0]
        quarter = (side_ref[1] + turn) % 4
        place = network.at[
            pl.ds(late * (BLOCKS // 2), depth), :, side,
            pl.ds(pl.multiple_of(quarter // 2 * half_rows, half_rows), half_rows),
            pl.ds(pl.multiple_of(quarter % 2 * width, width), width),
        ]
        return pltpu.make_async_copy(shares[k], place, net_sems.at[k])

    inputs = (
        pltpu.make_async_copy(press_hbm, pressure.at[0], in_sems.at[0]),
        pltpu.make_async_copy(forcing_hbm, forcing, in_sems.at[1]),
        pltpu.make_async_copy(fiber_hbm, fiber, in_sems.at[2]),
        pltpu.make_async_copy(state_hbm, table, in_sems.at[3]),
    )
    inputs[0].start()
    for k in range(2 * len(PIECES)):
        fetch(k).start()
    for copy in inputs[1:]:
        copy.start()

    def net(i, start, blocks):
        cols = pl.ds(start * SLICE, blocks * SLICE)
        return network[i, :, :, :, cols].reshape(SLICE, blocks * SLICE)

    def stored(n):
        return pltpu.make_async_copy(
            table.at[:, :, pl.ds(n * SLICE, SLICE)],
            table_hbm.at[:, :, pl.ds(n * SLICE, SLICE)],
            out_sems.at[n],
        )

    damp_sum[...] = jnp.zeros_like(damp_sum)
    stress_sum[...] = jnp.zeros_like(stress_sum)
    inputs[0].wait()
    for k in range(2 * len(PIECES)):
        fetch(k).wait()
    for iteration in range(ITERS):
        source = pressure.at[iteration]
        for step in range(BLOCKS):
            n = step
            cols = pl.ds(n * SLICE, SLICE)
            moved = dot_nt(source[:, pl.ds(n * SLICE, SENT * SLICE)], net(n, 0, SENT))
            for d in range(1, BLOCKS - SENT + 1):
                i = (n - d) % BLOCKS
                moved += dot_nn(source[:, pl.ds(i * SLICE, SLICE)], net(i, d, 1))
            if iteration == 0 and step == 0:
                inputs[1].wait()
                inputs[2].wait()
            damping = fiber[:, cols]
            bend = jnp.tanh(moved)
            if iteration < ITERS - 1:
                for a in range(3):
                    block = slice(a * rows, (a + 1) * rows)
                    value = (forcing[a, :, cols] - damping * bend[block]).astype(bf16)
                    pressure[iteration + 1, block, cols] = value
                    if n < SENT - 1:
                        pressure[iteration + 1, block, pl.ds(nodes + n * SLICE, SLICE)] = value
                continue
            if step == 0:
                inputs[3].wait()
            products = []
            for a in range(3):
                low = a * rows
                table[a, :, cols] = jnp.where(
                    occupied_ref[...] > 0, moved[low : low + cap], table[a, :, cols]
                )
                basis = moved[low + rows - 8 : low + rows]
                products += [basis * basis[k : k + 1] for k in range(1, COMPS + 1)]
            stored(n).start()
            products.append(jnp.zeros((256 - 24 * COMPS, SLICE), f32))
            weights = jnp.concatenate(products, axis=0).astype(bf16)
            damped = (jnp.concatenate([damping] * 3, axis=0) * (1.0 - bend * bend)).astype(bf16)
            damp_sum[...] += dot_nt(damped, weights)
            head = moved.astype(bf16)
            rest = (moved - head.astype(f32)).astype(bf16)
            load = loading_ref[:, cols]
            stress_sum[...] += dot_nt(head, load) + dot_nt(rest, load)

    def gathered(sums, shift):
        lanes = sums.shape[1]
        return (
            sums[0:rows]
            + pltpu.roll(sums[rows : 2 * rows], lanes - shift, 1)
            + pltpu.roll(sums[2 * rows : 3 * rows], lanes - 2 * shift, 1)
        )[:, 0:128]

    lane = lax.broadcasted_iota(jnp.int32, result_ref.shape, 1)
    stress = gathered(stress_sum[...], 8)
    damp = gathered(damp_sum[...], 8 * COMPS)
    result = jnp.where(lane < 8 * COMPS, damp, jnp.where(lane < 8 * COMPS + 8, stress, 0.0))
    result_ref[...] = result
    pick = pick_ref[...]
    head, middle, rest = three_parts(result)
    back_ref[...] = dot_nn(pick, head) + (dot_nn(pick, middle) + dot_nn(pick, rest))
    for n in range(BLOCKS):
        stored(n).wait()


def corner_kernel(own_ref, behind_ref, fixed_ref, own_data_ref, behind_data_ref, force_ref, block_ref, work, *, scale):
    lanes = work.shape[2]
    workers = own_ref.shape[0]
    total = jnp.zeros((16, NODE_DEV), f32)
    work[...] = jnp.zeros_like(work)
    for part, (arrived, data) in enumerate(((own_ref, own_data_ref), (behind_ref, behind_data_ref))):
        gx = data[0:1, :]
        gy = data[1:2, :]
        gz = data[2:3, :]
        volume = data[3:4, :] * scale
        node = data[4:5, :].astype(jnp.int32) - part * NODE_DEV
        worker = data[5:6, :].astype(jnp.int32)
        pick = (lax.broadcasted_iota(jnp.int32, (workers, lanes), 0) == worker).astype(f32)
        got = lax.dot_general(
            arrived[...], pick, (((0,), (0,)), ((), ())), preferred_element_type=f32, precision=highest
        )
        t = [fixed_ref[8 * j : 8 * j + 8, :] - got[8 * j : 8 * j + 8, :] for j in range(COMPS)]
        columns = (
            got[8 * COMPS : 8 * COMPS + 8, :],
            t[0] * gx + t[4] * gz + t[5] * gy,
            t[1] * gy + t[3] * gz + t[5] * gx,
            t[2] * gz + t[3] * gy + t[4] * gx,
        )
        for c, m in enumerate(columns):
            blocks = (
                m[1:2] * gx + m[5:6] * gz + m[6:7] * gy,
                m[2:3] * gy + m[4:5] * gz + m[6:7] * gx,
                m[3:4] * gz + m[4:5] * gy + m[5:6] * gx,
            )
            for a in range(3):
                r = a if c == 0 else 3 + 3 * a + c - 1
                work[part, r : r + 1, :] = blocks[a] * volume
        spread = (lax.broadcasted_iota(jnp.int32, (NODE_DEV, lanes), 0) == node).astype(f32)
        total += lax.dot_general(
            work[part], spread, (((1,), (1,)), ((), ())), preferred_element_type=f32, precision=highest
        )
    force_ref[...] = total[0:3]
    block_ref[...] = total[3:12]


def from_behind(block, axis, distance):
    devices = range(lax.axis_size(axis))
    route = [(i - distance, i) for i in devices if i - distance in devices]
    return lax.ppermute(block, axis, route)


RVE = ("z", "y", "core")
ALL = ("z", "y", "core", "blk")


def spread_network(compliance, ready):
    rows, nodes = compliance.shape
    ring = lax.axis_size("blk")
    width = SENT * SLICE // 2
    around = jnp.concatenate([compliance, compliance[:, : (SENT - 1) * SLICE]], axis=1)
    quarter = lax.axis_index("blk")
    start = (quarter // 2 * (rows // 2), lax.axis_index("z") * SLICE + quarter % 2 * width)
    part = lax.dynamic_slice(around, start, (rows // 2, width))
    depth, lines = lax.axis_size("z"), lax.axis_size("y")
    own = lax.all_to_all(
        jnp.broadcast_to(part[None], (depth * lines,) + part.shape), ("z", "y"),
        split_axis=0, concat_axis=0, tiled=True,
    ).reshape((depth, lines) + part.shape)

    def pass_on(value, step):
        return lax.ppermute(value, "blk", [(i, (i + step) % ring) for i in range(ring)])

    own, ready = lax.optimization_barrier((own, ready))
    near, far = own[: depth // 2], own[depth // 2 :]
    before_near, after_far = pass_on(near, 1), pass_on(far, -1)
    pieces = [own, before_near, pass_on(far, 1), pass_on(near, -1), after_far]
    pieces += [pass_on(before_near, 1), pass_on(after_far, -1)]
    return pieces, ready


def swap_cores(pieces, ready):
    last = list(lax.optimization_barrier((pieces[-2], pieces[-1], ready))[:2])
    pieces = pieces[:-2] + last
    return pieces + [lax.ppermute(piece, "core", [(0, 1), (1, 0)]) for piece in pieces]


def body(
    strain, fiber_coeff, gradients, volume, corners, rve_worker, rve_slot, slot_element,
    state_table, loading, compliance,
):
    elems = strain.shape[0]
    workers = lax.axis_size(RVE)
    columns = lax.axis_size("blk")
    cap = state_table.shape[0]
    nodes = compliance.shape[1]
    rows = round_up(cap + COMPS, 8)

    device_rank = lax.axis_index(ALL)
    worker_ids = jnp.arange(workers)

    send_pick = (worker_ids[:, None] == rve_worker[None, :]).astype(bf16)
    element_rows = jnp.concatenate([fiber_coeff, jnp.pad(strain, ((0, 0), (0, 128 - COMPS)))], axis=1)
    outgoing = jnp.dot(send_pick, element_rows).reshape(workers, 2, (nodes + 128) // 2)

    corner_data = jnp.concatenate(
        [
            jnp.transpose(gradients.reshape(4, 3, elems), (1, 0, 2)).reshape(3, 4 * elems),
            jnp.tile(volume, 4)[None, :],
            (corners - device_rank * NODE_DEV).reshape(1, 4 * elems).astype(f32),
            jnp.tile(rve_worker, 4)[None, :].astype(f32),
            jnp.zeros((2, 4 * elems), f32),
        ],
        axis=0,
    )
    behind_data = from_behind(corner_data, ALL, 1)

    occupied = slot_element >= 0
    home = jnp.where(occupied, slot_element // (elems * columns), -1)
    home_wide = jnp.pad(home, (0, rows - cap), constant_values=-1)
    slot_pick = (home_wide[:, None] == worker_ids[None, :]).astype(bf16)
    unit = (jnp.arange(rows)[:, None] - cap == jnp.arange(128)[None, :]).astype(f32)
    loading_rows = jnp.transpose(loading, (1, 0, 2))
    loading_wide = jnp.pad(loading_rows, ((0, 0), (0, 128 - COMPS), (0, 0)))
    loading_sums = jnp.pad(loading_rows, ((0, 0), (1, 1), (0, 0))).reshape(24, nodes)
    loading_sums = jnp.pad(loading_sums, ((8 * COMPS, 128 - 24 - 8 * COMPS), (0, 0)))
    states = jnp.transpose(state_table, (1, 0, 2))
    wide = nodes + (SENT - 1) * SLICE
    place = jnp.stack([lax.axis_index("core"), lax.axis_index("blk")]).astype(jnp.int32)

    pieces, ready = spread_network(
        compliance,
        (
            outgoing, corner_data, behind_data, slot_pick, slot_pick.T, occupied.astype(jnp.int32)[:, None],
            unit, loading_wide, loading_sums, place,
        ),
    )
    (
        outgoing, corner_data, behind_data, slot_pick, slot_give, occupied_rows,
        unit, loading_wide, loading_sums, place,
    ) = ready
    arrived = lax.all_to_all(outgoing, RVE, split_axis=0, concat_axis=0, tiled=True).reshape(workers, nodes + 128)

    press, forcing, fiber = pl.pallas_call(
        prepare_kernel,
        out_shape=(
            jax.ShapeDtypeStruct((3 * rows, wide), bf16),
            jax.ShapeDtypeStruct((3, rows, nodes), f32),
            jax.ShapeDtypeStruct((rows, nodes), f32),
        ),
        scratch_shapes=[pltpu.VMEM((rows, SLICE), f32)],
        name="prepare",
    )(slot_pick, unit, arrived, loading_wide, states)
    shares = swap_cores(pieces, press)
    vmem = pl.BlockSpec(memory_space=pltpu.VMEM)
    hbm = pl.BlockSpec(memory_space=pltpu.HBM)
    table, result, backward = pl.pallas_call(
        solve_kernel,
        out_shape=(
            jax.ShapeDtypeStruct((3, cap, nodes), f32),
            jax.ShapeDtypeStruct((rows, 128), f32),
            jax.ShapeDtypeStruct((workers, 128), f32),
        ),
        in_specs=[pl.BlockSpec(memory_space=pltpu.SMEM)] + [vmem] * 3 + [hbm] * (4 + 2 * len(PIECES)),
        out_specs=(hbm, vmem, vmem),
        scratch_shapes=[
            pltpu.VMEM((BLOCKS, lax.axis_size("y"), 2, compliance.shape[0], SENT * SLICE), bf16),
            pltpu.VMEM((ITERS, 3 * rows, wide), bf16),
            pltpu.VMEM((3, rows, nodes), f32),
            pltpu.VMEM((rows, nodes), f32),
            pltpu.VMEM((3, cap, nodes), f32),
            pltpu.VMEM((3 * rows, 256), f32),
            pltpu.VMEM((3 * rows, 128), f32),
            pltpu.SemaphoreType.DMA((2 * len(PIECES),)),
            pltpu.SemaphoreType.DMA((4,)),
            pltpu.SemaphoreType.DMA((BLOCKS,)),
        ],
        name="solve",
    )(
        place, slot_give, loading_sums,
        occupied_rows, press, forcing, fiber, states, *shares,
    )
    new_table = jnp.transpose(table, (1, 0, 2))

    returned = lax.all_to_all(backward, RVE, split_axis=0, concat_axis=0, tiled=True)
    fixed = jnp.pad(result[cap : cap + COMPS, 8 * COMPS + 1 : 8 * COMPS + 1 + COMPS], ((0, 0), (1, 1)))
    fixed, returned = lax.optimization_barrier((fixed.reshape(8 * COMPS, 1), returned))
    behind = from_behind(returned, ALL, 1)
    forces, blocks = pl.pallas_call(
        functools.partial(corner_kernel, scale=1.0 / (3 * nodes)),
        out_shape=(
            jax.ShapeDtypeStruct((3, NODE_DEV), f32),
            jax.ShapeDtypeStruct((9, NODE_DEV), f32),
        ),
        scratch_shapes=[pltpu.VMEM((2, 16, 4 * elems), f32)],
        compiler_params=pltpu.CompilerParams(vmem_limit_bytes=8 << 20),
        name="corners",
    )(returned, behind, fixed, corner_data, behind_data)
    return (new_table, forces, blocks)


def solution(mesh):
    workers, columns = mesh.devices.shape
    mesh = jax.sharding.Mesh(mesh.devices.reshape(8, workers // 16, 2, columns), ALL)
    return jax.shard_map(
        body,
        mesh=mesh,
        in_specs=(
            P(ALL, None),
            P(ALL, None),
            P(None, ALL),
            P(ALL),
            P(None, ALL),
            P(ALL),
            P(ALL),
            P(ALL),
            P(ALL, None, None),
            P(),
            P(RVE, None),
        ),
        out_specs=(P(ALL, None, None), P(None, ALL), P(None, ALL)),
        check_vma=False,
    )
```

```python
import functools

import jax
import jax.numpy as jnp
from jax import lax
from jax.experimental import pallas as pl
from jax.experimental.pallas import tpu as pltpu
from jax.sharding import PartitionSpec as P

ITERS = 3
NODE_DEV = 128
COMPS = 6
SLICE = 256
BLOCKS = 8
SENT = 5
PIECES = (0, 3, 1, 2)

highest = lax.Precision.HIGHEST
f32 = jnp.float32
bf16 = jnp.bfloat16


def round_up(value, step):
    return (value + step - 1) // step * step


def dot_nn(left, right):
    return lax.dot_general(left, right, (((1,), (0,)), ((), ())), preferred_element_type=f32)


def dot_nt(left, right):
    return lax.dot_general(left, right, (((1,), (1,)), ((), ())), preferred_element_type=f32)


def three_parts(value):
    head = value.astype(bf16)
    rest = value - head.astype(f32)
    middle = rest.astype(bf16)
    return head, middle, (rest - middle.astype(f32)).astype(bf16)


def prepare_kernel(pick_ref, unit_ref, arrived_ref, loading_ref, state_ref, press_ref, forcing_ref, fiber_ref, still):
    cap = state_ref.shape[1]
    rows = pick_ref.shape[0]
    nodes = state_ref.shape[2]
    pick = pick_ref[...]
    strain = (dot_nn(pick, arrived_ref[:, nodes:]) + unit_ref[...]).astype(bf16)
    still[...] = jnp.zeros_like(still)
    for start in range(0, nodes, SLICE):
        cols = pl.ds(start, SLICE)
        fiber = dot_nn(pick, arrived_ref[:, cols])
        fiber_ref[:, cols] = fiber
        for a in range(3):
            still[0:cap, :] = state_ref[a, :, cols]
            forcing = dot_nn(strain, loading_ref[a, :, cols])
            forcing_ref[a, :, cols] = forcing
            first = (forcing - fiber * jnp.tanh(still[...])).astype(bf16)
            press_ref[a * rows : (a + 1) * rows, cols] = first
            if nodes + start < press_ref.shape[1]:
                press_ref[a * rows : (a + 1) * rows, pl.ds(nodes + start, SLICE)] = first


def solve_kernel(
    side_ref, pick_ref, loading_ref, occupied_ref, press_hbm, forcing_hbm, fiber_hbm, state_hbm, *refs,
):
    shares = refs[: 2 * len(PIECES)]
    (
        table_hbm, result_ref, back_ref, network, pressure, forcing, fiber, table, damp_sum, stress_sum,
        net_sems, in_sems, out_sems,
    ) = refs[2 * len(PIECES) :]
    rows = fiber.shape[0]
    nodes = fiber.shape[1]
    cap = table.shape[1]
    half_rows = network.shape[3] // 2
    width = network.shape[4] // 2

    def fetch(k):
        side = side_ref[0] if k < len(PIECES) else 1 - side_ref[0]
        quarter = (side_ref[1] + PIECES[k % len(PIECES)]) % 4
        place = network.at[
            :, :, side,
            pl.ds(pl.multiple_of(quarter // 2 * half_rows, half_rows), half_rows),
            pl.ds(pl.multiple_of(quarter % 2 * width, width), width),
        ]
        return pltpu.make_async_copy(shares[k], place, net_sems.at[k])

    inputs = (
        pltpu.make_async_copy(press_hbm, pressure.at[0], in_sems.at[0]),
        pltpu.make_async_copy(forcing_hbm, forcing, in_sems.at[1]),
        pltpu.make_async_copy(fiber_hbm, fiber, in_sems.at[2]),
        pltpu.make_async_copy(state_hbm, table, in_sems.at[3]),
    )
    inputs[0].start()
    for k in range(2 * len(PIECES)):
        fetch(k).start()
    for copy in inputs[1:]:
        copy.start()

    def net(i, start, blocks):
        cols = pl.ds(start * SLICE, blocks * SLICE)
        return network[i, :, :, :, cols].reshape(SLICE, blocks * SLICE)

    def stored(n):
        return pltpu.make_async_copy(
            table.at[:, :, pl.ds(n * SLICE, SLICE)],
            table_hbm.at[:, :, pl.ds(n * SLICE, SLICE)],
            out_sems.at[n],
        )

    damp_sum[...] = jnp.zeros_like(damp_sum)
    stress_sum[...] = jnp.zeros_like(stress_sum)
    inputs[0].wait()
    for k in range(2 * len(PIECES)):
        fetch(k).wait()
    for iteration in range(ITERS):
        source = pressure.at[iteration]
        for step in range(BLOCKS):
            n = step
            cols = pl.ds(n * SLICE, SLICE)
            moved = dot_nt(source[:, pl.ds(n * SLICE, SENT * SLICE)], net(n, 0, SENT))
            for d in range(1, BLOCKS - SENT + 1):
                i = (n - d) % BLOCKS
                moved += dot_nn(source[:, pl.ds(i * SLICE, SLICE)], net(i, d, 1))
            if iteration == 0 and step == 0:
                inputs[1].wait()
                inputs[2].wait()
            damping = fiber[:, cols]
            bend = jnp.tanh(moved)
            if iteration < ITERS - 1:
                for a in range(3):
                    block = slice(a * rows, (a + 1) * rows)
                    value = (forcing[a, :, cols] - damping * bend[block]).astype(bf16)
                    pressure[iteration + 1, block, cols] = value
                    if n < SENT - 1:
                        pressure[iteration + 1, block, pl.ds(nodes + n * SLICE, SLICE)] = value
                continue
            if step == 0:
                inputs[3].wait()
            products = []
            for a in range(3):
                low = a * rows
                table[a, :, cols] = jnp.where(
                    occupied_ref[...] > 0, moved[low : low + cap], table[a, :, cols]
                )
                basis = moved[low + rows - 8 : low + rows]
                products += [basis * basis[k : k + 1] for k in range(1, COMPS + 1)]
            stored(n).start()
            products.append(jnp.zeros((256 - 24 * COMPS, SLICE), f32))
            weights = jnp.concatenate(products, axis=0).astype(bf16)
            damped = (jnp.concatenate([damping] * 3, axis=0) * (1.0 - bend * bend)).astype(bf16)
            damp_sum[...] += dot_nt(damped, weights)
            head = moved.astype(bf16)
            rest = (moved - head.astype(f32)).astype(bf16)
            load = loading_ref[:, cols]
            stress_sum[...] += dot_nt(head, load) + dot_nt(rest, load)

    def gathered(sums, shift):
        lanes = sums.shape[1]
        return (
            sums[0:rows]
            + pltpu.roll(sums[rows : 2 * rows], lanes - shift, 1)
            + pltpu.roll(sums[2 * rows : 3 * rows], lanes - 2 * shift, 1)
        )[:, 0:128]

    lane = lax.broadcasted_iota(jnp.int32, result_ref.shape, 1)
    stress = gathered(stress_sum[...], 8)
    damp = gathered(damp_sum[...], 8 * COMPS)
    result = jnp.where(lane < 8 * COMPS, damp, jnp.where(lane < 8 * COMPS + 8, stress, 0.0))
    result_ref[...] = result
    pick = pick_ref[...]
    head, middle, rest = three_parts(result)
    back_ref[...] = dot_nn(pick, head) + (dot_nn(pick, middle) + dot_nn(pick, rest))
    for n in range(BLOCKS):
        stored(n).wait()


def corner_kernel(own_ref, behind_ref, fixed_ref, own_data_ref, behind_data_ref, force_ref, block_ref, work, *, scale):
    lanes = work.shape[2]
    workers = own_ref.shape[0]
    total = jnp.zeros((16, NODE_DEV), f32)
    work[...] = jnp.zeros_like(work)
    for part, (arrived, data) in enumerate(((own_ref, own_data_ref), (behind_ref, behind_data_ref))):
        gx = data[0:1, :]
        gy = data[1:2, :]
        gz = data[2:3, :]
        volume = data[3:4, :] * scale
        node = data[4:5, :].astype(jnp.int32) - part * NODE_DEV
        worker = data[5:6, :].astype(jnp.int32)
        pick = (lax.broadcasted_iota(jnp.int32, (workers, lanes), 0) == worker).astype(f32)
        got = lax.dot_general(
            arrived[...], pick, (((0,), (0,)), ((), ())), preferred_element_type=f32, precision=highest
        )
        t = [fixed_ref[8 * j : 8 * j + 8, :] - got[8 * j : 8 * j + 8, :] for j in range(COMPS)]
        columns = (
            got[8 * COMPS : 8 * COMPS + 8, :],
            t[0] * gx + t[4] * gz + t[5] * gy,
            t[1] * gy + t[3] * gz + t[5] * gx,
            t[2] * gz + t[3] * gy + t[4] * gx,
        )
        for c, m in enumerate(columns):
            blocks = (
                m[1:2] * gx + m[5:6] * gz + m[6:7] * gy,
                m[2:3] * gy + m[4:5] * gz + m[6:7] * gx,
                m[3:4] * gz + m[4:5] * gy + m[5:6] * gx,
            )
            for a in range(3):
                r = a if c == 0 else 3 + 3 * a + c - 1
                work[part, r : r + 1, :] = blocks[a] * volume
        spread = (lax.broadcasted_iota(jnp.int32, (NODE_DEV, lanes), 0) == node).astype(f32)
        total += lax.dot_general(
            work[part], spread, (((1,), (1,)), ((), ())), preferred_element_type=f32, precision=highest
        )
    force_ref[...] = total[0:3]
    block_ref[...] = total[3:12]


def from_behind(block, axis, distance):
    devices = range(lax.axis_size(axis))
    route = [(i - distance, i) for i in devices if i - distance in devices]
    return lax.ppermute(block, axis, route)


RVE = ("z", "y", "core")
ALL = ("z", "y", "core", "blk")


def spread_network(compliance, ready):
    rows, nodes = compliance.shape
    ring = lax.axis_size("blk")
    width = SENT * SLICE // 2
    around = jnp.concatenate([compliance, compliance[:, : (SENT - 1) * SLICE]], axis=1)
    quarter = lax.axis_index("blk")
    start = (quarter // 2 * (rows // 2), lax.axis_index("z") * SLICE + quarter % 2 * width)
    part = lax.dynamic_slice(around, start, (rows // 2, width))
    depth, lines = lax.axis_size("z"), lax.axis_size("y")
    own = lax.all_to_all(
        jnp.broadcast_to(part[None], (depth * lines,) + part.shape), ("z", "y"),
        split_axis=0, concat_axis=0, tiled=True,
    ).reshape((depth, lines) + part.shape)

    def pass_on(value, step):
        return lax.ppermute(value, "blk", [(i, (i + step) % ring) for i in range(ring)])

    own, ready = lax.optimization_barrier((own, ready))
    before, after = pass_on(own, 1), pass_on(own, -1)
    pieces = [own, before, after, pass_on(before, 1)]
    return pieces, ready


def swap_cores(pieces, ready):
    pieces = pieces[:-1] + [lax.optimization_barrier((pieces[-1], ready))[0]]
    return pieces + [lax.ppermute(piece, "core", [(0, 1), (1, 0)]) for piece in pieces]


def body(
    strain, fiber_coeff, gradients, volume, corners, rve_worker, rve_slot, slot_element,
    state_table, loading, compliance,
):
    elems = strain.shape[0]
    workers = lax.axis_size(RVE)
    columns = lax.axis_size("blk")
    cap = state_table.shape[0]
    nodes = compliance.shape[1]
    rows = round_up(cap + COMPS, 8)

    device_rank = lax.axis_index(ALL)
    worker_ids = jnp.arange(workers)

    send_pick = (worker_ids[:, None] == rve_worker[None, :]).astype(bf16)
    element_rows = jnp.concatenate([fiber_coeff, jnp.pad(strain, ((0, 0), (0, 128 - COMPS)))], axis=1)
    outgoing = jnp.dot(send_pick, element_rows).reshape(workers, 2, (nodes + 128) // 2)

    occupied = slot_element >= 0
    home = jnp.where(occupied, slot_element // (elems * columns), -1)
    home_wide = jnp.pad(home, (0, rows - cap), constant_values=-1)
    slot_pick = (home_wide[:, None] == worker_ids[None, :]).astype(bf16)
    unit = (jnp.arange(rows)[:, None] - cap == jnp.arange(128)[None, :]).astype(f32)
    loading_rows = jnp.transpose(loading, (1, 0, 2))
    loading_wide = jnp.pad(loading_rows, ((0, 0), (0, 128 - COMPS), (0, 0)))
    loading_sums = jnp.pad(loading_rows, ((0, 0), (1, 1), (0, 0))).reshape(24, nodes)
    loading_sums = jnp.pad(loading_sums, ((8 * COMPS, 128 - 24 - 8 * COMPS), (0, 0)))
    states = jnp.transpose(state_table, (1, 0, 2))
    wide = nodes + (SENT - 1) * SLICE
    place = jnp.stack([lax.axis_index("core"), lax.axis_index("blk")]).astype(jnp.int32)

    pieces, ready = spread_network(
        compliance,
        (
            outgoing, slot_pick, slot_pick.T, occupied.astype(jnp.int32)[:, None],
            unit, loading_wide, loading_sums, place,
        ),
    )
    (
        outgoing, slot_pick, slot_give, occupied_rows,
        unit, loading_wide, loading_sums, place,
    ) = ready
    arrived = lax.all_to_all(outgoing, RVE, split_axis=0, concat_axis=0, tiled=True).reshape(workers, nodes + 128)

    press, forcing, fiber = pl.pallas_call(
        prepare_kernel,
        out_shape=(
            jax.ShapeDtypeStruct((3 * rows, wide), bf16),
            jax.ShapeDtypeStruct((3, rows, nodes), f32),
            jax.ShapeDtypeStruct((rows, nodes), f32),
        ),
        scratch_shapes=[pltpu.VMEM((rows, SLICE), f32)],
        name="prepare",
    )(slot_pick, unit, arrived, loading_wide, states)
    shares = swap_cores(pieces, press)
    vmem = pl.BlockSpec(memory_space=pltpu.VMEM)
    hbm = pl.BlockSpec(memory_space=pltpu.HBM)
    table, result, backward = pl.pallas_call(
        solve_kernel,
        out_shape=(
            jax.ShapeDtypeStruct((3, cap, nodes), f32),
            jax.ShapeDtypeStruct((rows, 128), f32),
            jax.ShapeDtypeStruct((workers, 128), f32),
        ),
        in_specs=[pl.BlockSpec(memory_space=pltpu.SMEM)] + [vmem] * 3 + [hbm] * (4 + 2 * len(PIECES)),
        out_specs=(hbm, vmem, vmem),
        scratch_shapes=[
            pltpu.VMEM((BLOCKS, lax.axis_size("y"), 2, compliance.shape[0], SENT * SLICE), bf16),
            pltpu.VMEM((ITERS, 3 * rows, wide), bf16),
            pltpu.VMEM((3, rows, nodes), f32),
            pltpu.VMEM((rows, nodes), f32),
            pltpu.VMEM((3, cap, nodes), f32),
            pltpu.VMEM((3 * rows, 256), f32),
            pltpu.VMEM((3 * rows, 128), f32),
            pltpu.SemaphoreType.DMA((2 * len(PIECES),)),
            pltpu.SemaphoreType.DMA((4,)),
            pltpu.SemaphoreType.DMA((BLOCKS,)),
        ],
        name="solve",
    )(
        place, slot_give, loading_sums,
        occupied_rows, press, forcing, fiber, states, *shares,
    )
    new_table = jnp.transpose(table, (1, 0, 2))

    returned = lax.all_to_all(backward, RVE, split_axis=0, concat_axis=0, tiled=True)
    result, gradients, volume, corners, rve_worker = lax.optimization_barrier(
        (result, gradients, volume, corners, rve_worker)
    )
    corner_data = jnp.concatenate(
        [
            jnp.transpose(gradients.reshape(4, 3, elems), (1, 0, 2)).reshape(3, 4 * elems),
            jnp.tile(volume, 4)[None, :],
            (corners - device_rank * NODE_DEV).reshape(1, 4 * elems).astype(f32),
            jnp.tile(rve_worker, 4)[None, :].astype(f32),
            jnp.zeros((2, 4 * elems), f32),
        ],
        axis=0,
    )
    behind_data = from_behind(corner_data, ALL, 1)

    fixed = jnp.pad(result[cap : cap + COMPS, 8 * COMPS + 1 : 8 * COMPS + 1 + COMPS], ((0, 0), (1, 1)))
    fixed, corner_data, behind_data, returned = lax.optimization_barrier(
        (fixed.reshape(8 * COMPS, 1), corner_data, behind_data, returned)
    )
    behind = from_behind(returned, ALL, 1)
    forces, blocks = pl.pallas_call(
        functools.partial(corner_kernel, scale=1.0 / (3 * nodes)),
        out_shape=(
            jax.ShapeDtypeStruct((3, NODE_DEV), f32),
            jax.ShapeDtypeStruct((9, NODE_DEV), f32),
        ),
        scratch_shapes=[pltpu.VMEM((2, 16, 4 * elems), f32)],
        compiler_params=pltpu.CompilerParams(vmem_limit_bytes=8 << 20),
        name="corners",
    )(returned, behind, fixed, corner_data, behind_data)
    return (new_table, forces, blocks)


def solution(mesh):
    workers, columns = mesh.devices.shape
    mesh = jax.sharding.Mesh(mesh.devices.reshape(8, workers // 16, 2, columns), ALL)
    return jax.shard_map(
        body,
        mesh=mesh,
        in_specs=(
            P(ALL, None),
            P(ALL, None),
            P(None, ALL),
            P(ALL),
            P(None, ALL),
            P(ALL),
            P(ALL),
            P(ALL),
            P(ALL, None, None),
            P(),
            P(RVE, None),
        ),
        out_specs=(P(ALL, None, None), P(None, ALL), P(None, ALL)),
        check_vma=False,
    )
```

```python
import functools

import jax
import jax.numpy as jnp
from jax import lax
from jax.experimental import pallas as pl
from jax.experimental.pallas import tpu as pltpu
from jax.sharding import PartitionSpec as P

ITERS = 3
NODE_DEV = 128
COMPS = 6
SLICE = 256
BLOCKS = 8
SENT = 5
PIECES = (0, 3, 1, 2)

highest = lax.Precision.HIGHEST
f32 = jnp.float32
bf16 = jnp.bfloat16


def round_up(value, step):
    return (value + step - 1) // step * step


def dot_nn(left, right):
    return lax.dot_general(left, right, (((1,), (0,)), ((), ())), preferred_element_type=f32)


def dot_tn(left, right):
    return lax.dot_general(left, right, (((0,), (0,)), ((), ())), preferred_element_type=f32)


def dot_nt(left, right):
    return lax.dot_general(left, right, (((1,), (1,)), ((), ())), preferred_element_type=f32)


def three_parts(value):
    head = value.astype(bf16)
    rest = value - head.astype(f32)
    middle = rest.astype(bf16)
    return head, middle, (rest - middle.astype(f32)).astype(bf16)


def prepare_kernel(pick_ref, unit_ref, arrived_ref, loading_ref, state_ref, press_ref, forcing_ref, fiber_ref, still):
    cap = state_ref.shape[1]
    rows = pick_ref.shape[0]
    nodes = state_ref.shape[2]
    pick = pick_ref[...]
    strain = (dot_nn(pick, arrived_ref[:, nodes:]) + unit_ref[...]).astype(bf16)
    still[...] = jnp.zeros_like(still)
    for start in range(0, nodes, SLICE):
        cols = pl.ds(start, SLICE)
        fiber = dot_nn(pick, arrived_ref[:, cols])
        fiber_ref[:, cols] = fiber
        for a in range(3):
            still[0:cap, :] = state_ref[a, :, cols]
            forcing = dot_nn(strain, loading_ref[a, :, cols])
            forcing_ref[a, :, cols] = forcing
            first = (forcing - fiber * jnp.tanh(still[...])).astype(bf16)
            press_ref[a * rows : (a + 1) * rows, cols] = first
            if nodes + start < press_ref.shape[1]:
                press_ref[a * rows : (a + 1) * rows, pl.ds(nodes + start, SLICE)] = first


def solve_kernel(
    side_ref, pick_ref, loading_hbm, press_hbm, forcing_hbm, fiber_hbm, state_hbm, *refs,
):
    shares = refs[: 2 * len(PIECES)]
    (
        table_hbm, result_ref, back_ref, network, pressure, forcing, fiber, table, loading, damp_sum, stress_sum,
        net_sems, in_sems, out_sems,
    ) = refs[2 * len(PIECES) :]
    rows = fiber.shape[0]
    nodes = fiber.shape[1]
    cap = table.shape[1]
    half_rows = network.shape[3] // 2
    width = network.shape[4] // 2

    def fetch(k):
        side = side_ref[0] if k < len(PIECES) else 1 - side_ref[0]
        quarter = (side_ref[1] + PIECES[k % len(PIECES)]) % 4
        place = network.at[
            :, :, side,
            pl.ds(pl.multiple_of(quarter // 2 * half_rows, half_rows), half_rows),
            pl.ds(pl.multiple_of(quarter % 2 * width, width), width),
        ]
        return pltpu.make_async_copy(shares[k], place, net_sems.at[k])

    inputs = (
        pltpu.make_async_copy(press_hbm, pressure.at[0], in_sems.at[0]),
        pltpu.make_async_copy(forcing_hbm, forcing, in_sems.at[1]),
        pltpu.make_async_copy(fiber_hbm, fiber, in_sems.at[2]),
        pltpu.make_async_copy(state_hbm, table, in_sems.at[3]),
        pltpu.make_async_copy(loading_hbm, loading, in_sems.at[4]),
    )
    inputs[0].start()
    for k in range(2 * len(PIECES)):
        fetch(k).start()
    for copy in inputs[1:]:
        copy.start()

    def net(i, start, blocks):
        cols = pl.ds(start * SLICE, blocks * SLICE)
        return network[i, :, :, :, cols].reshape(SLICE, blocks * SLICE)

    def stored(n):
        return pltpu.make_async_copy(
            table.at[:, :, pl.ds(n * SLICE, SLICE)],
            table_hbm.at[:, :, pl.ds(n * SLICE, SLICE)],
            out_sems.at[n],
        )

    occupied = jnp.sum(pick_ref[...].astype(f32), axis=1, keepdims=True)[0:cap] > 0.0
    damp_sum[...] = jnp.zeros_like(damp_sum)
    stress_sum[...] = jnp.zeros_like(stress_sum)
    inputs[0].wait()
    for k in range(2 * len(PIECES)):
        fetch(k).wait()
    for iteration in range(ITERS):
        source = pressure.at[iteration]
        for step in range(BLOCKS):
            n = step
            cols = pl.ds(n * SLICE, SLICE)
            moved = dot_nt(source[:, pl.ds(n * SLICE, SENT * SLICE)], net(n, 0, SENT))
            for d in range(1, BLOCKS - SENT + 1):
                i = (n - d) % BLOCKS
                moved += dot_nn(source[:, pl.ds(i * SLICE, SLICE)], net(i, d, 1))
            if iteration == 0 and step == 0:
                inputs[1].wait()
                inputs[2].wait()
            damping = fiber[:, cols]
            bend = jnp.tanh(moved)
            if iteration < ITERS - 1:
                for a in range(3):
                    block = slice(a * rows, (a + 1) * rows)
                    value = (forcing[a, :, cols] - damping * bend[block]).astype(bf16)
                    pressure[iteration + 1, block, cols] = value
                    if n < SENT - 1:
                        pressure[iteration + 1, block, pl.ds(nodes + n * SLICE, SLICE)] = value
                continue
            if step == 0:
                inputs[3].wait()
                inputs[4].wait()
            products = []
            for a in range(3):
                low = a * rows
                table[a, :, cols] = jnp.where(
                    occupied, moved[low : low + cap], table[a, :, cols]
                )
                basis = moved[low + rows - 8 : low + rows]
                products += [basis * basis[k : k + 1] for k in range(1, COMPS + 1)]
            stored(n).start()
            products.append(jnp.zeros((256 - 24 * COMPS, SLICE), f32))
            weights = jnp.concatenate(products, axis=0).astype(bf16)
            damped = (jnp.concatenate([damping] * 3, axis=0) * (1.0 - bend * bend)).astype(bf16)
            damp_sum[...] += dot_nt(damped, weights)
            head = moved.astype(bf16)
            rest = (moved - head.astype(f32)).astype(bf16)
            load = loading[:, cols]
            stress_sum[...] += dot_nt(head, load) + dot_nt(rest, load)

    def gathered(sums, shift):
        lanes = sums.shape[1]
        return (
            sums[0:rows]
            + pltpu.roll(sums[rows : 2 * rows], lanes - shift, 1)
            + pltpu.roll(sums[2 * rows : 3 * rows], lanes - 2 * shift, 1)
        )[:, 0:128]

    lane = lax.broadcasted_iota(jnp.int32, result_ref.shape, 1)
    stress = gathered(stress_sum[...], 8)
    damp = gathered(damp_sum[...], 8 * COMPS)
    result = jnp.where(lane < 8 * COMPS, damp, jnp.where(lane < 8 * COMPS + 8, stress, 0.0))
    result_ref[...] = result
    pick = pick_ref[...]
    head, middle, rest = three_parts(result)
    back_ref[...] = dot_tn(pick, head) + (dot_tn(pick, middle) + dot_tn(pick, rest))
    for n in range(BLOCKS):
        stored(n).wait()


def corner_kernel(own_ref, behind_ref, fixed_ref, own_data_ref, behind_data_ref, force_ref, block_ref, work, *, scale):
    lanes = work.shape[2]
    workers = own_ref.shape[0]
    total = jnp.zeros((16, NODE_DEV), f32)
    work[...] = jnp.zeros_like(work)
    for part, (arrived, data) in enumerate(((own_ref, own_data_ref), (behind_ref, behind_data_ref))):
        gx = data[0:1, :]
        gy = data[1:2, :]
        gz = data[2:3, :]
        volume = data[3:4, :] * scale
        node = data[4:5, :].astype(jnp.int32) - part * NODE_DEV
        worker = data[5:6, :].astype(jnp.int32)
        pick = (lax.broadcasted_iota(jnp.int32, (workers, lanes), 0) == worker).astype(f32)
        got = lax.dot_general(
            arrived[...], pick, (((0,), (0,)), ((), ())), preferred_element_type=f32, precision=highest
        )
        t = [fixed_ref[8 * j : 8 * j + 8, :] - got[8 * j : 8 * j + 8, :] for j in range(COMPS)]
        columns = (
            got[8 * COMPS : 8 * COMPS + 8, :],
            t[0] * gx + t[4] * gz + t[5] * gy,
            t[1] * gy + t[3] * gz + t[5] * gx,
            t[2] * gz + t[3] * gy + t[4] * gx,
        )
        for c, m in enumerate(columns):
            blocks = (
                m[1:2] * gx + m[5:6] * gz + m[6:7] * gy,
                m[2:3] * gy + m[4:5] * gz + m[6:7] * gx,
                m[3:4] * gz + m[4:5] * gy + m[5:6] * gx,
            )
            for a in range(3):
                r = a if c == 0 else 3 + 3 * a + c - 1
                work[part, r : r + 1, :] = blocks[a] * volume
        spread = (lax.broadcasted_iota(jnp.int32, (NODE_DEV, lanes), 0) == node).astype(f32)
        total += lax.dot_general(
            work[part], spread, (((1,), (1,)), ((), ())), preferred_element_type=f32, precision=highest
        )
    force_ref[...] = total[0:3]
    block_ref[...] = total[3:12]


def from_behind(block, axis, distance):
    devices = range(lax.axis_size(axis))
    route = [(i - distance, i) for i in devices if i - distance in devices]
    return lax.ppermute(block, axis, route)


RVE = ("z", "y", "core")
ALL = ("z", "y", "core", "blk")


def spread_network(compliance, ready):
    rows, nodes = compliance.shape
    ring = lax.axis_size("blk")
    width = SENT * SLICE // 2
    around = jnp.concatenate([compliance, compliance[:, : (SENT - 1) * SLICE]], axis=1)
    quarter = lax.axis_index("blk")
    start = (quarter // 2 * (rows // 2), lax.axis_index("z") * SLICE + quarter % 2 * width)
    part = lax.dynamic_slice(around, start, (rows // 2, width))
    depth, lines = lax.axis_size("z"), lax.axis_size("y")
    own = lax.all_to_all(
        jnp.broadcast_to(part[None], (depth * lines,) + part.shape), ("z", "y"),
        split_axis=0, concat_axis=0, tiled=True,
    ).reshape((depth, lines) + part.shape)

    def pass_on(value, step):
        return lax.ppermute(value, "blk", [(i, (i + step) % ring) for i in range(ring)])

    own, ready = lax.optimization_barrier((own, ready))
    before, after = pass_on(own, 1), pass_on(own, -1)
    pieces = [own, before, after, pass_on(before, 1)]
    return pieces, ready


def swap_cores(pieces, ready):
    pieces = pieces[:-1] + [lax.optimization_barrier((pieces[-1], ready))[0]]
    return pieces + [lax.ppermute(piece, "core", [(0, 1), (1, 0)]) for piece in pieces]


def body(
    strain, fiber_coeff, gradients, volume, corners, rve_worker, rve_slot, slot_element,
    state_table, loading, compliance,
):
    elems = strain.shape[0]
    workers = lax.axis_size(RVE)
    columns = lax.axis_size("blk")
    cap = state_table.shape[0]
    nodes = compliance.shape[1]
    rows = round_up(cap + COMPS, 8)

    device_rank = lax.axis_index(ALL)
    worker_ids = jnp.arange(workers)

    send_pick = (worker_ids[:, None] == rve_worker[None, :]).astype(bf16)
    element_rows = jnp.concatenate([fiber_coeff, jnp.pad(strain, ((0, 0), (0, 128 - COMPS)))], axis=1)
    outgoing = jnp.dot(send_pick, element_rows).reshape(workers, 2, (nodes + 128) // 2)

    occupied = slot_element >= 0
    home = jnp.where(occupied, slot_element // (elems * columns), -1)
    home_wide = jnp.pad(home, (0, rows - cap), constant_values=-1)
    slot_pick = (home_wide[:, None] == worker_ids[None, :]).astype(bf16)
    unit = (jnp.arange(rows)[:, None] - cap == jnp.arange(128)[None, :]).astype(f32)
    loading_rows = jnp.transpose(loading, (1, 0, 2))
    loading_wide = jnp.pad(loading_rows, ((0, 0), (0, 128 - COMPS), (0, 0)))
    loading_sums = jnp.pad(loading_rows, ((0, 0), (1, 1), (0, 0))).reshape(24, nodes)
    loading_sums = jnp.pad(loading_sums, ((8 * COMPS, 128 - 24 - 8 * COMPS), (0, 0)))
    states = jnp.transpose(state_table, (1, 0, 2))
    wide = nodes + (SENT - 1) * SLICE
    place = jnp.stack([lax.axis_index("core"), lax.axis_index("blk")]).astype(jnp.int32)

    pieces, ready = spread_network(
        compliance,
        (
            outgoing, slot_pick,
            unit, loading_wide, loading_sums, place,
        ),
    )
    (
        outgoing, slot_pick,
        unit, loading_wide, loading_sums, place,
    ) = ready
    arrived = lax.all_to_all(outgoing, RVE, split_axis=0, concat_axis=0, tiled=True).reshape(workers, nodes + 128)

    press, forcing, fiber = pl.pallas_call(
        prepare_kernel,
        out_shape=(
            jax.ShapeDtypeStruct((3 * rows, wide), bf16),
            jax.ShapeDtypeStruct((3, rows, nodes), f32),
            jax.ShapeDtypeStruct((rows, nodes), f32),
        ),
        scratch_shapes=[pltpu.VMEM((rows, SLICE), f32)],
        name="prepare",
    )(slot_pick, unit, arrived, loading_wide, states)
    shares = swap_cores(pieces, arrived)
    vmem = pl.BlockSpec(memory_space=pltpu.VMEM)
    hbm = pl.BlockSpec(memory_space=pltpu.HBM)
    table, result, backward = pl.pallas_call(
        solve_kernel,
        out_shape=(
            jax.ShapeDtypeStruct((3, cap, nodes), f32),
            jax.ShapeDtypeStruct((rows, 128), f32),
            jax.ShapeDtypeStruct((workers, 128), f32),
        ),
        in_specs=[pl.BlockSpec(memory_space=pltpu.SMEM)] + [vmem] + [hbm] * (5 + 2 * len(PIECES)),
        out_specs=(hbm, vmem, vmem),
        scratch_shapes=[
            pltpu.VMEM((BLOCKS, lax.axis_size("y"), 2, compliance.shape[0], SENT * SLICE), bf16),
            pltpu.VMEM((ITERS, 3 * rows, wide), bf16),
            pltpu.VMEM((3, rows, nodes), f32),
            pltpu.VMEM((rows, nodes), f32),
            pltpu.VMEM((3, cap, nodes), f32),
            pltpu.VMEM((128, nodes), bf16),
            pltpu.VMEM((3 * rows, 256), f32),
            pltpu.VMEM((3 * rows, 128), f32),
            pltpu.SemaphoreType.DMA((2 * len(PIECES),)),
            pltpu.SemaphoreType.DMA((5,)),
            pltpu.SemaphoreType.DMA((BLOCKS,)),
        ],
        name="solve",
    )(
        place, slot_pick, loading_sums, press, forcing, fiber, states, *shares,
    )
    new_table = jnp.transpose(table, (1, 0, 2))

    returned = lax.all_to_all(backward, RVE, split_axis=0, concat_axis=0, tiled=True)
    result, gradients, volume, corners, rve_worker = lax.optimization_barrier(
        (result, gradients, volume, corners, rve_worker)
    )
    corner_data = jnp.concatenate(
        [
            jnp.transpose(gradients.reshape(4, 3, elems), (1, 0, 2)).reshape(3, 4 * elems),
            jnp.tile(volume, 4)[None, :],
            (corners - device_rank * NODE_DEV).reshape(1, 4 * elems).astype(f32),
            jnp.tile(rve_worker, 4)[None, :].astype(f32),
            jnp.zeros((2, 4 * elems), f32),
        ],
        axis=0,
    )
    behind_data = from_behind(corner_data, ALL, 1)

    fixed = jnp.pad(result[cap : cap + COMPS, 8 * COMPS + 1 : 8 * COMPS + 1 + COMPS], ((0, 0), (1, 1)))
    fixed, corner_data, behind_data, returned = lax.optimization_barrier(
        (fixed.reshape(8 * COMPS, 1), corner_data, behind_data, returned)
    )
    behind = from_behind(returned, ALL, 1)
    forces, blocks = pl.pallas_call(
        functools.partial(corner_kernel, scale=1.0 / (3 * nodes)),
        out_shape=(
            jax.ShapeDtypeStruct((3, NODE_DEV), f32),
            jax.ShapeDtypeStruct((9, NODE_DEV), f32),
        ),
        scratch_shapes=[pltpu.VMEM((2, 16, 4 * elems), f32)],
        compiler_params=pltpu.CompilerParams(vmem_limit_bytes=8 << 20),
        name="corners",
    )(returned, behind, fixed, corner_data, behind_data)
    return (new_table, forces, blocks)


def solution(mesh):
    workers, columns = mesh.devices.shape
    mesh = jax.sharding.Mesh(mesh.devices.reshape(8, workers // 16, 2, columns), ALL)
    return jax.shard_map(
        body,
        mesh=mesh,
        in_specs=(
            P(ALL, None),
            P(ALL, None),
            P(None, ALL),
            P(ALL),
            P(None, ALL),
            P(ALL),
            P(ALL),
            P(ALL),
            P(ALL, None, None),
            P(),
            P(RVE, None),
        ),
        out_specs=(P(ALL, None, None), P(None, ALL), P(None, ALL)),
        check_vma=False,
    )
```

```python
import functools

import jax
import jax.numpy as jnp
from jax import lax
from jax.experimental import pallas as pl
from jax.experimental.pallas import tpu as pltpu
from jax.sharding import PartitionSpec as P

ITERS = 3
NODE_DEV = 128
COMPS = 6
SLICE = 256
BLOCKS = 8
SENT = 5
PIECES = (0, 3, 1, 2)

highest = lax.Precision.HIGHEST
f32 = jnp.float32
bf16 = jnp.bfloat16


def round_up(value, step):
    return (value + step - 1) // step * step


def dot_nn(left, right):
    return lax.dot_general(left, right, (((1,), (0,)), ((), ())), preferred_element_type=f32)


def dot_tn(left, right):
    return lax.dot_general(left, right, (((0,), (0,)), ((), ())), preferred_element_type=f32)


def dot_nt(left, right):
    return lax.dot_general(left, right, (((1,), (1,)), ((), ())), preferred_element_type=f32)


def three_parts(value):
    head = value.astype(bf16)
    rest = value - head.astype(f32)
    middle = rest.astype(bf16)
    return head, middle, (rest - middle.astype(f32)).astype(bf16)


def prepare_kernel(
    pick_ref, unit_ref, strain_ref, arrived_ref, loading_ref, state_ref, press_ref, forcing_ref, fiber_ref, still
):
    cap = state_ref.shape[1]
    rows = pick_ref.shape[0]
    pick = pick_ref[...]
    strain = (dot_nn(pick, strain_ref[...]) + unit_ref[...]).astype(bf16)[:, : loading_ref.shape[1]]
    fiber = dot_nn(pick, arrived_ref[...])
    fiber_ref[...] = fiber
    still[...] = jnp.zeros_like(still)
    for a in range(3):
        still[0:cap, :] = state_ref[a]
        forcing = dot_nn(strain, loading_ref[a])
        forcing_ref[a] = forcing
        press_ref[a * rows : (a + 1) * rows, :] = (forcing - fiber * jnp.tanh(still[...])).astype(bf16)


def solve_kernel(
    side_ref, pick_ref, loading_hbm, press_hbm, forcing_hbm, fiber_hbm, state_hbm, *refs,
):
    shares = refs[: 2 * len(PIECES)]
    (
        table_hbm, result_ref, back_ref, network, pressure, forcing, fiber, table, loading, damp_sum, stress_sum,
        net_sems, in_sems, out_sems,
    ) = refs[2 * len(PIECES) :]
    rows = fiber.shape[0]
    nodes = fiber.shape[1]
    cap = table.shape[1]
    half_rows = network.shape[3] // 2
    width = network.shape[4] // 2

    def fetch(k):
        side = side_ref[0] if k < len(PIECES) else 1 - side_ref[0]
        quarter = (side_ref[1] + PIECES[k % len(PIECES)]) % 4
        place = network.at[
            :, :, side,
            pl.ds(pl.multiple_of(quarter // 2 * half_rows, half_rows), half_rows),
            pl.ds(pl.multiple_of(quarter % 2 * width, width), width),
        ]
        return pltpu.make_async_copy(shares[k], place, net_sems.at[k])

    inputs = (
        pltpu.make_async_copy(press_hbm, pressure.at[0, :, pl.ds(0, nodes)], in_sems.at[0]),
        pltpu.make_async_copy(forcing_hbm, forcing, in_sems.at[1]),
        pltpu.make_async_copy(fiber_hbm, fiber, in_sems.at[2]),
        pltpu.make_async_copy(state_hbm, table, in_sems.at[3]),
        pltpu.make_async_copy(loading_hbm, loading, in_sems.at[4]),
    )
    over = pressure.shape[2] - nodes
    wrap = pltpu.make_async_copy(
        press_hbm.at[:, pl.ds(0, over)], pressure.at[0, :, pl.ds(nodes, over)], in_sems.at[5]
    )
    inputs[0].start()
    wrap.start()
    for k in range(2 * len(PIECES)):
        fetch(k).start()
    for copy in inputs[1:]:
        copy.start()

    def net(i, start, blocks):
        cols = pl.ds(start * SLICE, blocks * SLICE)
        return network[i, :, :, :, cols].reshape(SLICE, blocks * SLICE)

    def stored(n):
        return pltpu.make_async_copy(
            table.at[:, :, pl.ds(n * SLICE, SLICE)],
            table_hbm.at[:, :, pl.ds(n * SLICE, SLICE)],
            out_sems.at[n],
        )

    occupied = jnp.sum(pick_ref[...].astype(f32), axis=1, keepdims=True)[0:cap] > 0.0
    damp_sum[...] = jnp.zeros_like(damp_sum)
    stress_sum[...] = jnp.zeros_like(stress_sum)
    inputs[0].wait()
    wrap.wait()
    for k in range(2 * len(PIECES)):
        fetch(k).wait()

    def advance(iteration, n, moved):
        cols = pl.ds(n * SLICE, SLICE)
        damping = fiber[:, cols]
        bend = jnp.tanh(moved)
        for a in range(3):
            block = slice(a * rows, (a + 1) * rows)
            value = (forcing[a, :, cols] - damping * bend[block]).astype(bf16)
            pressure[iteration + 1, block, cols] = value
            if n < SENT - 1:
                pressure[iteration + 1, block, pl.ds(nodes + n * SLICE, SLICE)] = value

    for iteration in range(ITERS):
        source = pressure.at[iteration]
        held = []
        for step in range(BLOCKS):
            n = step
            cols = pl.ds(n * SLICE, SLICE)
            moved = dot_nt(source[:, pl.ds(n * SLICE, SENT * SLICE)], net(n, 0, SENT))
            for d in range(1, BLOCKS - SENT + 1):
                i = (n - d) % BLOCKS
                moved += dot_nn(source[:, pl.ds(i * SLICE, SLICE)], net(i, d, 1))
            if iteration < ITERS - 1:
                held.append((n, moved))
                if iteration == 0 and step == 1:
                    inputs[1].wait()
                    inputs[2].wait()
                if iteration > 0 or step > 0:
                    for k, value in held:
                        advance(iteration, k, value)
                    held = []
                continue
            damping = fiber[:, cols]
            bend = jnp.tanh(moved)
            if step == 0:
                inputs[3].wait()
                inputs[4].wait()
            products = []
            for a in range(3):
                low = a * rows
                table[a, :, cols] = jnp.where(
                    occupied, moved[low : low + cap], table[a, :, cols]
                )
                basis = moved[low + rows - 8 : low + rows]
                products += [basis * basis[k : k + 1] for k in range(1, COMPS + 1)]
            stored(n).start()
            products.append(jnp.zeros((256 - 24 * COMPS, SLICE), f32))
            weights = jnp.concatenate(products, axis=0).astype(bf16)
            damped = (jnp.concatenate([damping] * 3, axis=0) * (1.0 - bend * bend)).astype(bf16)
            damp_sum[...] += dot_nt(damped, weights)
            head = moved.astype(bf16)
            rest = (moved - head.astype(f32)).astype(bf16)
            load = loading[:, cols]
            stress_sum[...] += dot_nt(head, load) + dot_nt(rest, load)

    def gathered(sums, shift):
        lanes = sums.shape[1]
        return (
            sums[0:rows]
            + pltpu.roll(sums[rows : 2 * rows], lanes - shift, 1)
            + pltpu.roll(sums[2 * rows : 3 * rows], lanes - 2 * shift, 1)
        )[:, 0:128]

    lane = lax.broadcasted_iota(jnp.int32, result_ref.shape, 1)
    stress = gathered(stress_sum[...], 8)
    damp = gathered(damp_sum[...], 8 * COMPS)
    result = jnp.where(lane < 8 * COMPS, damp, jnp.where(lane < 8 * COMPS + 8, stress, 0.0))
    result_ref[...] = result
    pick = pick_ref[...]
    head, middle, rest = three_parts(result)
    back_ref[...] = dot_tn(pick, head) + (dot_tn(pick, middle) + dot_tn(pick, rest))
    for n in range(BLOCKS):
        stored(n).wait()


def corner_kernel(own_ref, behind_ref, fixed_ref, own_data_ref, behind_data_ref, force_ref, block_ref, work, *, scale):
    lanes = work.shape[2]
    workers = own_ref.shape[0]
    total = jnp.zeros((16, NODE_DEV), f32)
    work[...] = jnp.zeros_like(work)
    for part, (arrived, data) in enumerate(((own_ref, own_data_ref), (behind_ref, behind_data_ref))):
        gx = data[0:1, :]
        gy = data[1:2, :]
        gz = data[2:3, :]
        volume = data[3:4, :] * scale
        node = data[4:5, :].astype(jnp.int32) - part * NODE_DEV
        worker = data[5:6, :].astype(jnp.int32)
        pick = (lax.broadcasted_iota(jnp.int32, (workers, lanes), 0) == worker).astype(f32)
        got = lax.dot_general(
            arrived[...], pick, (((0,), (0,)), ((), ())), preferred_element_type=f32, precision=highest
        )
        t = [fixed_ref[8 * j : 8 * j + 8, :] - got[8 * j : 8 * j + 8, :] for j in range(COMPS)]
        columns = (
            got[8 * COMPS : 8 * COMPS + 8, :],
            t[0] * gx + t[4] * gz + t[5] * gy,
            t[1] * gy + t[3] * gz + t[5] * gx,
            t[2] * gz + t[3] * gy + t[4] * gx,
        )
        for c, m in enumerate(columns):
            blocks = (
                m[1:2] * gx + m[5:6] * gz + m[6:7] * gy,
                m[2:3] * gy + m[4:5] * gz + m[6:7] * gx,
                m[3:4] * gz + m[4:5] * gy + m[5:6] * gx,
            )
            for a in range(3):
                r = a if c == 0 else 3 + 3 * a + c - 1
                work[part, r : r + 1, :] = blocks[a] * volume
        spread = (lax.broadcasted_iota(jnp.int32, (NODE_DEV, lanes), 0) == node).astype(f32)
        total += lax.dot_general(
            work[part], spread, (((1,), (1,)), ((), ())), preferred_element_type=f32, precision=highest
        )
    force_ref[...] = total[0:3]
    block_ref[...] = total[3:12]


def from_behind(block, axis, distance):
    devices = range(lax.axis_size(axis))
    route = [(i - distance, i) for i in devices if i - distance in devices]
    return lax.ppermute(block, axis, route)


RVE = ("z", "y", "core")
ALL = ("z", "y", "core", "blk")


def spread_network(compliance, ready):
    rows, nodes = compliance.shape
    ring = lax.axis_size("blk")
    width = SENT * SLICE // 2
    around = jnp.concatenate([compliance, compliance[:, : (SENT - 1) * SLICE]], axis=1)
    quarter = lax.axis_index("blk")
    start = (quarter // 2 * (rows // 2), lax.axis_index("z") * SLICE + quarter % 2 * width)
    part = lax.dynamic_slice(around, start, (rows // 2, width))
    depth, lines = lax.axis_size("z"), lax.axis_size("y")
    own = lax.all_to_all(
        jnp.broadcast_to(part[None], (depth * lines,) + part.shape), ("z", "y"),
        split_axis=0, concat_axis=0, tiled=True,
    ).reshape((depth, lines) + part.shape)

    def pass_on(value, step):
        return lax.ppermute(value, "blk", [(i, (i + step) % ring) for i in range(ring)])

    own, ready = lax.optimization_barrier((own, ready))
    before, after = pass_on(own, 1), pass_on(own, -1)
    pieces = [own, before, after, pass_on(before, 1)]
    return pieces, ready


def swap_cores(pieces, ready):
    pieces = pieces[:-1] + [lax.optimization_barrier((pieces[-1], ready))[0]]
    return pieces + [lax.ppermute(piece, "core", [(0, 1), (1, 0)]) for piece in pieces]


def body(
    strain, fiber_coeff, gradients, volume, corners, rve_worker, rve_slot, slot_element,
    state_table, loading, compliance,
):
    elems = strain.shape[0]
    workers = lax.axis_size(RVE)
    columns = lax.axis_size("blk")
    cap = state_table.shape[0]
    nodes = compliance.shape[1]
    rows = round_up(cap + COMPS, 8)

    device_rank = lax.axis_index(ALL)
    worker_ids = jnp.arange(workers)

    send_pick = (worker_ids[:, None] == rve_worker[None, :]).astype(bf16)
    element_rows = jnp.concatenate([fiber_coeff, jnp.pad(strain, ((0, 0), (0, 128 - COMPS)))], axis=1)
    outgoing = jnp.dot(send_pick, element_rows).reshape(workers, 2, (nodes + 128) // 2)

    occupied = slot_element >= 0
    home = jnp.where(occupied, slot_element // (elems * columns), -1)
    home_wide = jnp.pad(home, (0, rows - cap), constant_values=-1)
    slot_pick = (home_wide[:, None] == worker_ids[None, :]).astype(bf16)
    unit = (jnp.arange(rows)[:, None] - cap == jnp.arange(128)[None, :]).astype(f32)
    loading_rows = jnp.transpose(loading, (1, 0, 2))
    loading_wide = jnp.pad(loading_rows, ((0, 0), (0, 16 - COMPS), (0, 0)))
    loading_sums = jnp.pad(loading_rows, ((0, 0), (1, 1), (0, 0))).reshape(24, nodes)
    loading_sums = jnp.pad(loading_sums, ((8 * COMPS, 128 - 24 - 8 * COMPS), (0, 0)))
    states = jnp.transpose(state_table, (1, 0, 2))
    wide = nodes + (SENT - 1) * SLICE
    place = jnp.stack([lax.axis_index("core"), lax.axis_index("blk")]).astype(jnp.int32)

    pieces, ready = spread_network(
        compliance,
        (
            outgoing, slot_pick,
            unit, loading_wide, loading_sums, place,
        ),
    )
    (
        outgoing, slot_pick,
        unit, loading_wide, loading_sums, place,
    ) = ready
    arrived = lax.all_to_all(outgoing, RVE, split_axis=0, concat_axis=0, tiled=True).reshape(workers, nodes + 128)

    press, forcing, fiber = pl.pallas_call(
        prepare_kernel,
        grid=(nodes // SLICE,),
        in_specs=[
            pl.BlockSpec((rows, workers), lambda i: (0, 0)),
            pl.BlockSpec((rows, 128), lambda i: (0, 0)),
            pl.BlockSpec((workers, 128), lambda i: (0, nodes // 128)),
            pl.BlockSpec((workers, SLICE), lambda i: (0, i)),
            pl.BlockSpec((3, 16, SLICE), lambda i: (0, 0, i)),
            pl.BlockSpec((3, cap, SLICE), lambda i: (0, 0, i)),
        ],
        out_specs=(
            pl.BlockSpec((3 * rows, SLICE), lambda i: (0, i)),
            pl.BlockSpec((3, rows, SLICE), lambda i: (0, 0, i)),
            pl.BlockSpec((rows, SLICE), lambda i: (0, i)),
        ),
        out_shape=(
            jax.ShapeDtypeStruct((3 * rows, nodes), bf16),
            jax.ShapeDtypeStruct((3, rows, nodes), f32),
            jax.ShapeDtypeStruct((rows, nodes), f32),
        ),
        scratch_shapes=[pltpu.VMEM((rows, SLICE), f32)],
        name="prepare",
    )(slot_pick, unit, arrived, arrived, loading_wide, states)
    shares = swap_cores(pieces, arrived)
    vmem = pl.BlockSpec(memory_space=pltpu.VMEM)
    hbm = pl.BlockSpec(memory_space=pltpu.HBM)
    table, result, backward = pl.pallas_call(
        solve_kernel,
        out_shape=(
            jax.ShapeDtypeStruct((3, cap, nodes), f32),
            jax.ShapeDtypeStruct((rows, 128), f32),
            jax.ShapeDtypeStruct((workers, 128), f32),
        ),
        in_specs=[pl.BlockSpec(memory_space=pltpu.SMEM)] + [vmem] + [hbm] * (5 + 2 * len(PIECES)),
        out_specs=(hbm, vmem, vmem),
        scratch_shapes=[
            pltpu.VMEM((BLOCKS, lax.axis_size("y"), 2, compliance.shape[0], SENT * SLICE), bf16),
            pltpu.VMEM((ITERS, 3 * rows, wide), bf16),
            pltpu.VMEM((3, rows, nodes), f32),
            pltpu.VMEM((rows, nodes), f32),
            pltpu.VMEM((3, cap, nodes), f32),
            pltpu.VMEM((128, nodes), bf16),
            pltpu.VMEM((3 * rows, 256), f32),
            pltpu.VMEM((3 * rows, 128), f32),
            pltpu.SemaphoreType.DMA((2 * len(PIECES),)),
            pltpu.SemaphoreType.DMA((6,)),
            pltpu.SemaphoreType.DMA((BLOCKS,)),
        ],
        name="solve",
    )(
        place, slot_pick, loading_sums, press, forcing, fiber, states, *shares,
    )
    new_table = jnp.transpose(table, (1, 0, 2))

    returned = lax.all_to_all(backward, RVE, split_axis=0, concat_axis=0, tiled=True)
    result, gradients, volume, corners, rve_worker = lax.optimization_barrier(
        (result, gradients, volume, corners, rve_worker)
    )
    corner_data = jnp.concatenate(
        [
            jnp.transpose(gradients.reshape(4, 3, elems), (1, 0, 2)).reshape(3, 4 * elems),
            jnp.tile(volume, 4)[None, :],
            (corners - device_rank * NODE_DEV).reshape(1, 4 * elems).astype(f32),
            jnp.tile(rve_worker, 4)[None, :].astype(f32),
            jnp.zeros((2, 4 * elems), f32),
        ],
        axis=0,
    )
    behind_data = from_behind(corner_data, ALL, 1)

    fixed = jnp.pad(result[cap : cap + COMPS, 8 * COMPS + 1 : 8 * COMPS + 1 + COMPS], ((0, 0), (1, 1)))
    fixed, corner_data, behind_data, returned = lax.optimization_barrier(
        (fixed.reshape(8 * COMPS, 1), corner_data, behind_data, returned)
    )
    behind = from_behind(returned, ALL, 1)
    forces, blocks = pl.pallas_call(
        functools.partial(corner_kernel, scale=1.0 / (3 * nodes)),
        out_shape=(
            jax.ShapeDtypeStruct((3, NODE_DEV), f32),
            jax.ShapeDtypeStruct((9, NODE_DEV), f32),
        ),
        scratch_shapes=[pltpu.VMEM((2, 16, 4 * elems), f32)],
        compiler_params=pltpu.CompilerParams(vmem_limit_bytes=8 << 20),
        name="corners",
    )(returned, behind, fixed, corner_data, behind_data)
    return (new_table, forces, blocks)


def solution(mesh):
    workers, columns = mesh.devices.shape
    mesh = jax.sharding.Mesh(mesh.devices.reshape(8, workers // 16, 2, columns), ALL)
    return jax.shard_map(
        body,
        mesh=mesh,
        in_specs=(
            P(ALL, None),
            P(ALL, None),
            P(None, ALL),
            P(ALL),
            P(None, ALL),
            P(ALL),
            P(ALL),
            P(ALL),
            P(ALL, None, None),
            P(),
            P(RVE, None),
        ),
        out_specs=(P(ALL, None, None), P(None, ALL), P(None, ALL)),
        check_vma=False,
    )
```

```python
import functools

import jax
import jax.numpy as jnp
from jax import lax
from jax.experimental import pallas as pl
from jax.experimental.pallas import tpu as pltpu
from jax.sharding import PartitionSpec as P

ITERS = 3
NODE_DEV = 128
COMPS = 6
SLICE = 256
BLOCKS = 8
SENT = 5
PIECES = (0, 3, 1, 2)

highest = lax.Precision.HIGHEST
f32 = jnp.float32
bf16 = jnp.bfloat16


def round_up(value, step):
    return (value + step - 1) // step * step


def dot_nn(left, right):
    return lax.dot_general(left, right, (((1,), (0,)), ((), ())), preferred_element_type=f32)


def dot_tn(left, right):
    return lax.dot_general(left, right, (((0,), (0,)), ((), ())), preferred_element_type=f32)


def dot_nt(left, right):
    return lax.dot_general(left, right, (((1,), (1,)), ((), ())), preferred_element_type=f32)


def three_parts(value):
    head = value.astype(bf16)
    rest = value - head.astype(f32)
    middle = rest.astype(bf16)
    return head, middle, (rest - middle.astype(f32)).astype(bf16)


def prepare_kernel(
    pick_ref, unit_ref, arrived_ref, loading_ref, state_ref, press_ref, forcing_ref, fiber_ref, still
):
    cap = state_ref.shape[1]
    rows = pick_ref.shape[0]
    nodes = state_ref.shape[2]
    pick = pick_ref[...]
    strain = (dot_nn(pick, arrived_ref[:, nodes:]) + unit_ref[...]).astype(bf16)[:, : loading_ref.shape[1]]
    still[...] = jnp.zeros_like(still)
    for start in range(0, nodes, SLICE):
        cols = pl.ds(start, SLICE)
        fiber = dot_nn(pick, arrived_ref[:, cols])
        fiber_ref[:, cols] = fiber
        for a in range(3):
            still[0:cap, :] = state_ref[a, :, cols]
            forcing = dot_nn(strain, loading_ref[a, :, cols])
            forcing_ref[a, :, cols] = forcing
            press_ref[a * rows : (a + 1) * rows, cols] = (
                forcing - fiber * jnp.tanh(still[...])
            ).astype(bf16)


def solve_kernel(
    side_ref, pick_ref, loading_hbm, press_hbm, forcing_hbm, fiber_hbm, state_hbm, *refs,
):
    shares = refs[: 2 * len(PIECES)]
    (
        table_hbm, result_ref, back_ref, network, pressure, forcing, fiber, table, loading, damp_sum, stress_sum,
        net_sems, in_sems, out_sems,
    ) = refs[2 * len(PIECES) :]
    rows = fiber.shape[0]
    nodes = fiber.shape[1]
    cap = table.shape[1]
    half_rows = network.shape[3] // 2
    width = network.shape[4] // 2

    def fetch(k):
        side = side_ref[0] if k < len(PIECES) else 1 - side_ref[0]
        quarter = (side_ref[1] + PIECES[k % len(PIECES)]) % 4
        place = network.at[
            :, :, side,
            pl.ds(pl.multiple_of(quarter // 2 * half_rows, half_rows), half_rows),
            pl.ds(pl.multiple_of(quarter % 2 * width, width), width),
        ]
        return pltpu.make_async_copy(shares[k], place, net_sems.at[k])

    inputs = (
        pltpu.make_async_copy(press_hbm, pressure.at[0, :, pl.ds(0, nodes)], in_sems.at[0]),
        pltpu.make_async_copy(forcing_hbm, forcing, in_sems.at[1]),
        pltpu.make_async_copy(fiber_hbm, fiber, in_sems.at[2]),
        pltpu.make_async_copy(state_hbm, table, in_sems.at[3]),
        pltpu.make_async_copy(loading_hbm, loading, in_sems.at[4]),
    )
    over = pressure.shape[2] - nodes
    wrap = pltpu.make_async_copy(
        press_hbm.at[:, pl.ds(0, over)], pressure.at[0, :, pl.ds(nodes, over)], in_sems.at[5]
    )
    inputs[0].start()
    wrap.start()
    for k in range(2 * len(PIECES)):
        fetch(k).start()
    for copy in inputs[1:]:
        copy.start()

    def net(i, start, blocks):
        cols = pl.ds(start * SLICE, blocks * SLICE)
        return network[i, :, :, :, cols].reshape(SLICE, blocks * SLICE)

    def stored(n):
        return pltpu.make_async_copy(
            table.at[:, :, pl.ds(n * SLICE, SLICE)],
            table_hbm.at[:, :, pl.ds(n * SLICE, SLICE)],
            out_sems.at[n],
        )

    occupied = jnp.sum(pick_ref[...].astype(f32), axis=1, keepdims=True)[0:cap] > 0.0
    damp_sum[...] = jnp.zeros_like(damp_sum)
    stress_sum[...] = jnp.zeros_like(stress_sum)
    inputs[0].wait()
    wrap.wait()
    for k in range(2 * len(PIECES)):
        fetch(k).wait()

    def advance(iteration, n, moved):
        cols = pl.ds(n * SLICE, SLICE)
        damping = fiber[:, cols]
        bend = jnp.tanh(moved)
        for a in range(3):
            block = slice(a * rows, (a + 1) * rows)
            value = (forcing[a, :, cols] - damping * bend[block]).astype(bf16)
            pressure[iteration + 1, block, cols] = value
            if n < SENT - 1:
                pressure[iteration + 1, block, pl.ds(nodes + n * SLICE, SLICE)] = value

    for iteration in range(ITERS):
        source = pressure.at[iteration]
        held = []
        for step in range(BLOCKS):
            n = step
            cols = pl.ds(n * SLICE, SLICE)
            moved = dot_nt(source[:, pl.ds(n * SLICE, SENT * SLICE)], net(n, 0, SENT))
            for d in range(1, BLOCKS - SENT + 1):
                i = (n - d) % BLOCKS
                moved += dot_nn(source[:, pl.ds(i * SLICE, SLICE)], net(i, d, 1))
            if iteration < ITERS - 1:
                held.append((n, moved))
                if iteration == 0 and step == 1:
                    inputs[1].wait()
                    inputs[2].wait()
                if iteration > 0 or step > 0:
                    for k, value in held:
                        advance(iteration, k, value)
                    held = []
                continue
            damping = fiber[:, cols]
            bend = jnp.tanh(moved)
            if step == 0:
                inputs[3].wait()
                inputs[4].wait()
            products = []
            for a in range(3):
                low = a * rows
                table[a, :, cols] = jnp.where(
                    occupied, moved[low : low + cap], table[a, :, cols]
                )
                basis = moved[low + rows - 8 : low + rows]
                products += [basis * basis[k : k + 1] for k in range(1, COMPS + 1)]
            stored(n).start()
            products.append(jnp.zeros((256 - 24 * COMPS, SLICE), f32))
            weights = jnp.concatenate(products, axis=0).astype(bf16)
            damped = (jnp.concatenate([damping] * 3, axis=0) * (1.0 - bend * bend)).astype(bf16)
            damp_sum[...] += dot_nt(damped, weights)
            head = moved.astype(bf16)
            rest = (moved - head.astype(f32)).astype(bf16)
            load = loading[:, cols]
            stress_sum[...] += dot_nt(head, load) + dot_nt(rest, load)

    def gathered(sums, shift):
        lanes = sums.shape[1]
        return (
            sums[0:rows]
            + pltpu.roll(sums[rows : 2 * rows], lanes - shift, 1)
            + pltpu.roll(sums[2 * rows : 3 * rows], lanes - 2 * shift, 1)
        )[:, 0:128]

    lane = lax.broadcasted_iota(jnp.int32, result_ref.shape, 1)
    stress = gathered(stress_sum[...], 8)
    damp = gathered(damp_sum[...], 8 * COMPS)
    result = jnp.where(lane < 8 * COMPS, damp, jnp.where(lane < 8 * COMPS + 8, stress, 0.0))
    result_ref[...] = result
    pick = pick_ref[...]
    head, middle, rest = three_parts(result)
    back_ref[...] = dot_tn(pick, head) + (dot_tn(pick, middle) + dot_tn(pick, rest))
    for n in range(BLOCKS):
        stored(n).wait()


def corner_kernel(own_ref, behind_ref, fixed_ref, own_data_ref, behind_data_ref, force_ref, block_ref, work, *, scale):
    lanes = work.shape[2]
    workers = own_ref.shape[0]
    total = jnp.zeros((16, NODE_DEV), f32)
    work[...] = jnp.zeros_like(work)
    for part, (arrived, data) in enumerate(((own_ref, own_data_ref), (behind_ref, behind_data_ref))):
        gx = data[0:1, :]
        gy = data[1:2, :]
        gz = data[2:3, :]
        volume = data[3:4, :] * scale
        node = data[4:5, :].astype(jnp.int32) - part * NODE_DEV
        worker = data[5:6, :].astype(jnp.int32)
        pick = (lax.broadcasted_iota(jnp.int32, (workers, lanes), 0) == worker).astype(f32)
        got = lax.dot_general(
            arrived[...], pick, (((0,), (0,)), ((), ())), preferred_element_type=f32, precision=highest
        )
        t = [fixed_ref[8 * j : 8 * j + 8, :] - got[8 * j : 8 * j + 8, :] for j in range(COMPS)]
        columns = (
            got[8 * COMPS : 8 * COMPS + 8, :],
            t[0] * gx + t[4] * gz + t[5] * gy,
            t[1] * gy + t[3] * gz + t[5] * gx,
            t[2] * gz + t[3] * gy + t[4] * gx,
        )
        for c, m in enumerate(columns):
            blocks = (
                m[1:2] * gx + m[5:6] * gz + m[6:7] * gy,
                m[2:3] * gy + m[4:5] * gz + m[6:7] * gx,
                m[3:4] * gz + m[4:5] * gy + m[5:6] * gx,
            )
            for a in range(3):
                r = a if c == 0 else 3 + 3 * a + c - 1
                work[part, r : r + 1, :] = blocks[a] * volume
        spread = (lax.broadcasted_iota(jnp.int32, (NODE_DEV, lanes), 0) == node).astype(f32)
        total += lax.dot_general(
            work[part], spread, (((1,), (1,)), ((), ())), preferred_element_type=f32, precision=highest
        )
    force_ref[...] = total[0:3]
    block_ref[...] = total[3:12]


def from_behind(block, axis, distance):
    devices = range(lax.axis_size(axis))
    route = [(i - distance, i) for i in devices if i - distance in devices]
    return lax.ppermute(block, axis, route)


RVE = ("z", "y", "core")
ALL = ("z", "y", "core", "blk")


def spread_network(compliance, ready):
    rows, nodes = compliance.shape
    ring = lax.axis_size("blk")
    width = SENT * SLICE // 2
    around = jnp.concatenate([compliance, compliance[:, : (SENT - 1) * SLICE]], axis=1)
    quarter = lax.axis_index("blk")
    start = (quarter // 2 * (rows // 2), lax.axis_index("z") * SLICE + quarter % 2 * width)
    part = lax.dynamic_slice(around, start, (rows // 2, width))
    depth, lines = lax.axis_size("z"), lax.axis_size("y")
    own = lax.all_to_all(
        jnp.broadcast_to(part[None], (depth * lines,) + part.shape), ("z", "y"),
        split_axis=0, concat_axis=0, tiled=True,
    ).reshape((depth, lines) + part.shape)

    def pass_on(value, step):
        return lax.ppermute(value, "blk", [(i, (i + step) % ring) for i in range(ring)])

    own, ready = lax.optimization_barrier((own, ready))
    before, after = pass_on(own, 1), pass_on(own, -1)
    pieces = [own, before, after, pass_on(before, 1)]
    return pieces, ready


def swap_cores(pieces, ready):
    pieces = pieces[:-1] + [lax.optimization_barrier((pieces[-1], ready))[0]]
    return pieces + [lax.ppermute(piece, "core", [(0, 1), (1, 0)]) for piece in pieces]


def body(
    strain, fiber_coeff, gradients, volume, corners, rve_worker, rve_slot, slot_element,
    state_table, loading, compliance,
):
    elems = strain.shape[0]
    workers = lax.axis_size(RVE)
    columns = lax.axis_size("blk")
    cap = state_table.shape[0]
    nodes = compliance.shape[1]
    rows = round_up(cap + COMPS, 8)

    device_rank = lax.axis_index(ALL)
    worker_ids = jnp.arange(workers)

    send_pick = (worker_ids[:, None] == rve_worker[None, :]).astype(bf16)
    element_rows = jnp.concatenate([fiber_coeff, jnp.pad(strain, ((0, 0), (0, 128 - COMPS)))], axis=1)
    outgoing = jnp.dot(send_pick, element_rows).reshape(workers, 2, (nodes + 128) // 2)

    occupied = slot_element >= 0
    home = jnp.where(occupied, slot_element // (elems * columns), -1)
    home_wide = jnp.pad(home, (0, rows - cap), constant_values=-1)
    slot_pick = (home_wide[:, None] == worker_ids[None, :]).astype(bf16)
    unit = (jnp.arange(rows)[:, None] - cap == jnp.arange(128)[None, :]).astype(f32)
    loading_rows = jnp.transpose(loading, (1, 0, 2))
    loading_wide = jnp.pad(loading_rows, ((0, 0), (0, 16 - COMPS), (0, 0)))
    loading_sums = jnp.pad(loading_rows, ((0, 0), (1, 1), (0, 0))).reshape(24, nodes)
    loading_sums = jnp.pad(loading_sums, ((8 * COMPS, 128 - 24 - 8 * COMPS), (0, 0)))
    states = jnp.transpose(state_table, (1, 0, 2))
    wide = nodes + (SENT - 1) * SLICE
    place = jnp.stack([lax.axis_index("core"), lax.axis_index("blk")]).astype(jnp.int32)

    pieces, ready = spread_network(
        compliance,
        (
            outgoing, slot_pick,
            unit, loading_wide, loading_sums, place,
        ),
    )
    (
        outgoing, slot_pick,
        unit, loading_wide, loading_sums, place,
    ) = ready
    arrived = lax.all_to_all(outgoing, RVE, split_axis=0, concat_axis=0, tiled=True).reshape(workers, nodes + 128)

    press, forcing, fiber = pl.pallas_call(
        prepare_kernel,
        out_shape=(
            jax.ShapeDtypeStruct((3 * rows, nodes), bf16),
            jax.ShapeDtypeStruct((3, rows, nodes), f32),
            jax.ShapeDtypeStruct((rows, nodes), f32),
        ),
        scratch_shapes=[pltpu.VMEM((rows, SLICE), f32)],
        name="prepare",
    )(slot_pick, unit, arrived, loading_wide, states)
    shares = swap_cores(pieces, arrived)
    vmem = pl.BlockSpec(memory_space=pltpu.VMEM)
    hbm = pl.BlockSpec(memory_space=pltpu.HBM)
    table, result, backward = pl.pallas_call(
        solve_kernel,
        out_shape=(
            jax.ShapeDtypeStruct((3, cap, nodes), f32),
            jax.ShapeDtypeStruct((rows, 128), f32),
            jax.ShapeDtypeStruct((workers, 128), f32),
        ),
        in_specs=[pl.BlockSpec(memory_space=pltpu.SMEM)] + [vmem] + [hbm] * (5 + 2 * len(PIECES)),
        out_specs=(hbm, vmem, vmem),
        scratch_shapes=[
            pltpu.VMEM((BLOCKS, lax.axis_size("y"), 2, compliance.shape[0], SENT * SLICE), bf16),
            pltpu.VMEM((ITERS, 3 * rows, wide), bf16),
            pltpu.VMEM((3, rows, nodes), f32),
            pltpu.VMEM((rows, nodes), f32),
            pltpu.VMEM((3, cap, nodes), f32),
            pltpu.VMEM((128, nodes), bf16),
            pltpu.VMEM((3 * rows, 256), f32),
            pltpu.VMEM((3 * rows, 128), f32),
            pltpu.SemaphoreType.DMA((2 * len(PIECES),)),
            pltpu.SemaphoreType.DMA((6,)),
            pltpu.SemaphoreType.DMA((BLOCKS,)),
        ],
        name="solve",
    )(
        place, slot_pick, loading_sums, press, forcing, fiber, states, *shares,
    )
    new_table = jnp.transpose(table, (1, 0, 2))

    returned = lax.all_to_all(backward, RVE, split_axis=0, concat_axis=0, tiled=True)
    result, gradients, volume, corners, rve_worker = lax.optimization_barrier(
        (result, gradients, volume, corners, rve_worker)
    )
    corner_data = jnp.concatenate(
        [
            jnp.transpose(gradients.reshape(4, 3, elems), (1, 0, 2)).reshape(3, 4 * elems),
            jnp.tile(volume, 4)[None, :],
            (corners - device_rank * NODE_DEV).reshape(1, 4 * elems).astype(f32),
            jnp.tile(rve_worker, 4)[None, :].astype(f32),
            jnp.zeros((2, 4 * elems), f32),
        ],
        axis=0,
    )
    behind_data = from_behind(corner_data, ALL, 1)

    fixed = jnp.pad(result[cap : cap + COMPS, 8 * COMPS + 1 : 8 * COMPS + 1 + COMPS], ((0, 0), (1, 1)))
    fixed, corner_data, behind_data, returned = lax.optimization_barrier(
        (fixed.reshape(8 * COMPS, 1), corner_data, behind_data, returned)
    )
    behind = from_behind(returned, ALL, 1)
    forces, blocks = pl.pallas_call(
        functools.partial(corner_kernel, scale=1.0 / (3 * nodes)),
        out_shape=(
            jax.ShapeDtypeStruct((3, NODE_DEV), f32),
            jax.ShapeDtypeStruct((9, NODE_DEV), f32),
        ),
        scratch_shapes=[pltpu.VMEM((2, 16, 4 * elems), f32)],
        compiler_params=pltpu.CompilerParams(vmem_limit_bytes=8 << 20),
        name="corners",
    )(returned, behind, fixed, corner_data, behind_data)
    return (new_table, forces, blocks)


def solution(mesh):
    workers, columns = mesh.devices.shape
    mesh = jax.sharding.Mesh(mesh.devices.reshape(8, workers // 16, 2, columns), ALL)
    return jax.shard_map(
        body,
        mesh=mesh,
        in_specs=(
            P(ALL, None),
            P(ALL, None),
            P(None, ALL),
            P(ALL),
            P(None, ALL),
            P(ALL),
            P(ALL),
            P(ALL),
            P(ALL, None, None),
            P(),
            P(RVE, None),
        ),
        out_specs=(P(ALL, None, None), P(None, ALL), P(None, ALL)),
        check_vma=False,
    )
```
